512 devices in a mesh: row: 32 (over z, x), col: 16 (over y, core).
Axes of the slice: x: 4, y: 8, z: 8, core: 2. Of those that a mesh axis runs over, the one named last changes fastest.
Arguments:
- rhs: float32 [512, 64, 128], P(('row', 'col')), may hold values from -16 to 16
- item_factors: bfloat16 [1024, 64, 128], P('col'), may hold values from -0.125 to 0.125
- slot_users: int32 [32, 16, 96], P('row', 'col'), may hold values from 0 to 15, as said below
- slot_items: int32 [32, 16, 96], P('row', 'col'), may hold values from 0 to 63
- slot_counts: int32 [32, 16], P('row', 'col'), may hold values from 12 to 96, as said below
- mask_words: int32 [32, 16, 96, 16, 128], P('row', 'col'), may hold values from 0 to 255
- self_tiles: int32 [512, 128, 128], P(('row', 'col')), may hold values from 0 to 3, as said below
- next_tiles: int32 [512, 128, 128], P(('row', 'col')), may hold values from 0 to 3, as said below
Outputs:
- solution: float32 [512, 64, 128], P(('row', 'col'))
- residual: float32 [512, 64, 128], P(('row', 'col'))
The draws below stay inside these ranges and needn't reach their ends.
Inputs may be any that keep to these rules, and one draw needn't show every extreme that they name: `slot_users`: on each grid cell the 96 slots name distinct pairs of user block and item block. Some grid cells use all 96 slots; slots at positions slot_counts or later are ignored. `self_tiles`: most weights are zero. `next_tiles`: most weights are zero.
All inputs are finite; a program needn't handle non-finite values.
Results may differ from the reference program's by a relative error of at most 0.018.
Values may be sent and summed in bfloat16 or wider, within the bound.
A program may use at most 64 MiB of HBM per device.

```python
import jax
import jax.numpy as jnp
from jax import lax

BLOCK = 128
K = 64
ITERS = 2
UB_DEV = 1
IBC = 64
S_CAP = 96
GRID_ROWS = 32
GRID_COLS = 16
ROW_BLOCKS = 16
USER_BLOCKS = 512
USERS = 65536
ITEM_BLOCKS = 1024


def draw_rhs(key, part):
    position = (jnp.arange(USER_BLOCKS, dtype=jnp.float32)[:, None, None] * BLOCK + jnp.arange(BLOCK, dtype=jnp.float32)[None, None, :]) / USERS
    base = jnp.clip(jax.random.normal(key, (USER_BLOCKS, K, BLOCK), jnp.float32), -5.0, 5.0)
    return base * jnp.power(3.0, position)


def slot_table(key):
    inner = jax.random.fold_in(key, 11)
    keys = jax.random.split(inner, GRID_ROWS * GRID_COLS)
    table = jax.vmap(lambda single: jax.random.permutation(single, ROW_BLOCKS * IBC))(keys)
    return table[:, :S_CAP].reshape(GRID_ROWS, GRID_COLS, S_CAP).astype(jnp.int32)


def draw_slot_users(key, part):
    return slot_table(key) // IBC


def draw_slot_items(key, part):
    return slot_table(key) % IBC


def draw_slot_counts(key, part):
    first, second, third = jax.random.split(jax.random.fold_in(key, 5), 3)
    light = jax.random.randint(first, (GRID_ROWS, GRID_COLS), S_CAP // 8, S_CAP // 2 + 1)
    heavy = jax.random.randint(second, (GRID_ROWS, GRID_COLS), 0, 8) == 0
    chosen = jax.random.randint(third, (), 0, GRID_ROWS * GRID_COLS)
    forced = jnp.arange(GRID_ROWS * GRID_COLS).reshape(GRID_ROWS, GRID_COLS) == chosen
    return jnp.where(heavy | forced, S_CAP, light).astype(jnp.int32)


def sparse_weights(key):
    values = jax.random.randint(key, (USER_BLOCKS, BLOCK, BLOCK), 0, 32)
    return jnp.maximum(values - 28, 0).astype(jnp.int32)


def draw_self_tiles(key, part):
    return sparse_weights(jax.random.fold_in(key, 21))


def draw_next_tiles(key, part):
    return sparse_weights(jax.random.fold_in(key, 31))


def plant(values, rng, low, largest):
    extent = values.shape
    spot = [jax.random.randint(jax.random.fold_in(rng, axis), (), 0, extent[axis]) for axis in range(len(extent))]
    values = values.at[tuple(spot)].set(low)
    longest = extent.index(max(extent))
    spot[longest] = (spot[longest] + 1) % extent[longest]
    return values.at[tuple(spot)].set(largest)


def steps_of(own_key, extent, shards, low, top_value):
    def one(dim, shards_of):
        heights = jax.random.uniform(jax.random.fold_in(jax.random.fold_in(own_key, 6), dim), (shards_of,), jnp.float32, low / len(shards), top_value / len(shards))
        return jnp.repeat(jnp.exp(heights), extent[dim] // shards_of).reshape((-1,) + (1,) * (len(extent) - dim - 1))

    factor_of = one(*shards[0])
    for cut in shards[1:]:
        factor_of = factor_of * one(*cut)
    return factor_of


def centred(key, shape, width, reach, cuts=(), kind=jnp.bfloat16):
    array = jax.random.normal(key, shape, jnp.float32) * width
    if len(cuts) > 0:
        array = steps_of(key, shape, cuts, -0.22, 0.18) * array
    return jnp.clip(array, min=-reach, max=reach).astype(kind)


def setup_inputs(seed: int = 0) -> dict:
    key_of = jax.random.split(jax.random.key(seed), 9)
    return {
        "rhs": draw_rhs(jax.random.fold_in(key_of[8], 71), 0),
        "item_factors": centred(key_of[1], (ITEM_BLOCKS, K, BLOCK), 2048 ** -0.5, 0.125, ((0, 16),)),
        "slot_users": draw_slot_users(jax.random.fold_in(key_of[8], 71), 0),
        "slot_items": draw_slot_items(jax.random.fold_in(key_of[8], 71), 0),
        "slot_counts": draw_slot_counts(jax.random.fold_in(key_of[8], 71), 0),
        "mask_words": plant(jax.random.randint(key_of[5], (GRID_ROWS, GRID_COLS, S_CAP, BLOCK // 8, BLOCK), 0, 256), jax.random.fold_in(key_of[5], 1), 0, 255).astype(jnp.int32),
        "self_tiles": draw_self_tiles(jax.random.fold_in(key_of[8], 71), 0),
        "next_tiles": draw_next_tiles(jax.random.fold_in(key_of[8], 71), 0),
    }


graph_weight = 0.01
ridge_weight = 0.5


def unpack_masks(words):
    shifts = jnp.arange(8, dtype=jnp.int32)
    bits = jnp.right_shift(words[:, :, None, :], shifts[None, None, :, None]) & 1
    return bits.reshape(words.shape[0], words.shape[1] * 8, words.shape[2]).astype(jnp.float32)


def data_term(shared, item_factors, slot_users, slot_items, slot_counts, mask_words):
    grid_rows, grid_cols, capacity = slot_users.shape
    row_blocks = shared.shape[0] // grid_rows
    item_blocks = item_factors.shape[0] // grid_cols
    group = 16 if capacity % 16 == 0 else capacity

    def device(acc, place):
        row_index = place // grid_cols
        col_index = place % grid_cols
        users = (slot_users[row_index, col_index] + row_index * row_blocks).astype(jnp.int32)
        items = (slot_items[row_index, col_index] + col_index * item_blocks).astype(jnp.int32)
        words = mask_words[row_index, col_index]
        count = slot_counts[row_index, col_index]
        trips = (count + group - 1) // group

        def turn(index, inner):
            start = (index * group).astype(jnp.int32)
            part_users = lax.dynamic_slice_in_dim(users, start, group)
            part_items = lax.dynamic_slice_in_dim(items, start, group)
            part_words = lax.dynamic_slice_in_dim(words, start, group)
            valid = ((start + jnp.arange(group, dtype=jnp.int32)) < count).astype(jnp.float32)
            left = item_factors[part_items].astype(jnp.float32)
            right = shared[part_users].astype(jnp.float32)
            scores = jnp.einsum("sdi,sdu->siu", left, right)
            tiles = (scores * unpack_masks(part_words) * valid[:, None, None]).astype(jnp.bfloat16)
            return inner.at[part_users].add(jnp.einsum("siu,sdi->sdu", tiles.astype(jnp.float32), left))

        return lax.fori_loop(0, trips, turn, acc), None

    start_acc = jnp.zeros(shared.shape, jnp.float32)
    places = jnp.arange(grid_rows * grid_cols, dtype=jnp.int32)
    total, unused = lax.scan(device, start_acc, places)
    return total


def graph_term(shared, self_tiles, next_tiles, row_blocks):
    blocks = shared.shape[0]
    local = jnp.arange(blocks, dtype=jnp.int32) % row_blocks
    keep = (local < row_blocks - 1).astype(jnp.float32)
    own = shared.astype(jnp.float32)
    after = jnp.roll(own, -1, axis=0)
    before = jnp.roll(own, 1, axis=0)
    sym = (self_tiles + jnp.swapaxes(self_tiles, 1, 2)).astype(jnp.float32)
    edges = next_tiles.astype(jnp.float32) * keep[:, None, None]
    back = jnp.roll(edges, 1, axis=0)
    degree = jnp.sum(sym, axis=2) + jnp.sum(edges, axis=2) + jnp.sum(back, axis=1)
    result = degree[:, None, :] * own - jnp.einsum("buv,bdv->bdu", sym, own)
    result = result - jnp.einsum("buv,bdv->bdu", edges, after)
    return result - jnp.einsum("buv,bdu->bdv", back, before)


def reference(rhs, item_factors, slot_users, slot_items, slot_counts, mask_words, self_tiles, next_tiles):
    row_blocks = UB_DEV * GRID_COLS

    def apply(vector):
        shared = vector.astype(jnp.bfloat16)
        data = data_term(shared, item_factors, slot_users, slot_items, slot_counts, mask_words)
        graph = graph_term(shared, self_tiles, next_tiles, row_blocks)
        return data + graph_weight * graph + ridge_weight * vector

    solution = jnp.zeros_like(rhs)
    residual = rhs
    direction = rhs
    norm_now = jnp.sum(residual * residual)
    for iteration in range(ITERS):
        image = apply(direction)
        alpha = norm_now / jnp.sum(direction * image)
        solution = solution + alpha * direction
        residual = residual - alpha * image
        norm_next = jnp.sum(residual * residual)
        direction = residual + (norm_next / norm_now) * direction
        norm_now = norm_next
    return solution, residual
```

```python
import functools

import jax
import jax.numpy as jnp
from jax import lax
from jax.experimental import pallas as pl
from jax.experimental.pallas import tpu as pltpu
from jax.sharding import PartitionSpec as P

GRAPH = 0.01
RIDGE = 0.5
UNROLL = 8
f32, bf16, i32 = jnp.float32, jnp.bfloat16, jnp.int32


def far_first(cols):
    chips = cols // 2
    order = sorted(range(1, chips), key=lambda o: -min(o, chips - o))
    return order


def kernel(
    rows,
    cols,
    rhs_ref,
    items_hbm,
    users_ref,
    slot_items_ref,
    count_ref,
    words_hbm,
    self_hbm,
    next_hbm,
    sol_ref,
    res_ref,
    a_ref,
    at_ref,
    w_ref,
    m_ref,
    t_ref,
    s_ref,
    r1_ref,
    r2_ref,
    x1_ref,
    x2_ref,
    y1_ref,
    y2_ref,
    self_ref,
    next_ref,
    sym_ref,
    e_ref,
    et_ref,
    code_ref,
    code_sm,
    p1_ref,
    p2_ref,
    p3_ref,
    local_sem,
    g1_send,
    g1_recv,
    x1_send,
    x1_recv,
    p1_send,
    p1_recv,
    g2_send,
    g2_recv,
    x2_send,
    x2_recv,
    p2_send,
    p2_recv,
    p3_send,
    p3_recv,
):
    slots = w_ref.shape[0]
    blocks = a_ref.shape[0]
    me = lax.axis_index("col")
    my_row = lax.axis_index("row")
    my_chip, my_core = me // 2, me % 2
    chips = cols // 2

    def peers():
        for o in far_first(cols):
            chip = lax.rem(my_chip + o, chips)
            for c in (0, 1):
                yield 2 * o + c - 2, chip * 2 + lax.rem(my_core + c, 2)
        yield 2 * chips - 2, my_chip * 2 + 1 - my_core

    loads = [
        pltpu.make_async_copy(self_hbm.at[0], self_ref, local_sem.at[0]),
        pltpu.make_async_copy(next_hbm.at[0], next_ref, local_sem.at[1]),
        pltpu.make_async_copy(items_hbm, a_ref, local_sem.at[2]),
        pltpu.make_async_copy(words_hbm.at[0, 0], w_ref, local_sem.at[3]),
    ]
    for load in loads:
        load.start()

    barrier = pltpu.get_barrier_semaphore()
    for _, peer in peers():
        pl.semaphore_signal(
            barrier, inc=1, device_id={"col": peer}, device_id_type=pl.DeviceIdType.MESH
        )
    for o in range(1, rows):
        pl.semaphore_signal(
            barrier,
            inc=1,
            device_id={"row": lax.rem(my_row + o, rows)},
            device_id_type=pl.DeviceIdType.MESH,
        )

    rhs = rhs_ref[0]
    r1_ref[pl.ds(me, 1)] = rhs.astype(bf16)[None]
    r1_ref[cols] = jnp.zeros(r1_ref.shape[1:], bf16)
    r2_ref[cols] = jnp.zeros(r2_ref.shape[1:], bf16)
    s_ref[0] = jnp.zeros(s_ref.shape[1:], f32)

    lane = lax.broadcasted_iota(i32, (1, 128), 1)
    code_ref[...] = jnp.broadcast_to((cols + 1) * 8192 + lane * 64, (8, 128))
    slot = lax.broadcasted_iota(i32, (1, slots), 1)
    user = jnp.where(slot < count_ref[0, 0], users_ref[0], cols)
    code_ref[0:1, 0:slots] = user * 8192 + slot * 64 + slot_items_ref[0]
    across = jnp.broadcast_to(code_ref[0:1, :].astype(f32), (128, 128))
    down = across.T
    rank = jnp.sum(jnp.where(across < down, 1.0, 0.0), axis=1, keepdims=True)
    lanes = lax.broadcasted_iota(i32, (128, 128), 1).astype(f32)
    ordered = jnp.sum(jnp.where(rank == lanes, down, 0.0), axis=0, keepdims=True)
    upto = jnp.sum(jnp.where(down < (lanes + 1.0) * 8192.0, 1.0, 0.0), axis=0, keepdims=True)
    before = jnp.sum(jnp.where(down < lanes * 8192.0, 1.0, 0.0), axis=0, keepdims=True)
    code_ref[0:1, :] = ordered.astype(i32)
    code_ref[1:2, :] = jnp.where(upto > before, upto, 0.0).astype(i32)
    to_scalars = pltpu.make_async_copy(code_ref, code_sm, local_sem.at[4])
    to_scalars.start()

    pl.semaphore_wait(barrier, cols - 1 + rows - 1)

    def gather(r_ref, send, recv):
        return [
            pltpu.make_async_remote_copy(
                src_ref=r_ref.at[me],
                dst_ref=r_ref.at[me],
                send_sem=send.at[i],
                recv_sem=recv.at[me],
                device_id={"col": peer},
                device_id_type=pl.DeviceIdType.MESH,
            )
            for i, peer in peers()
        ]

    def arrive(ref, recv):
        for i, peer in peers():
            pltpu.make_async_copy(ref.at[peer], ref.at[peer], recv.at[peer]).wait()

    sent1 = gather(r1_ref, g1_send, g1_recv)
    for copy in sent1:
        copy.start()

    loads[0].wait()
    loads[1].wait()
    first = self_ref[...].astype(f32)
    sym = first + first.T
    keep = jnp.where(me < cols - 1, 1.0, 0.0)
    edges = next_ref[...].astype(f32) * keep
    edges_t = edges.T
    there_degree = jnp.sum(edges, axis=0, keepdims=True)
    here_degree = jnp.sum(sym, axis=0, keepdims=True) + jnp.sum(edges_t, axis=0, keepdims=True)
    sym_ref[...] = sym.astype(bf16)
    e_ref[...] = edges.astype(bf16)
    et_ref[...] = edges_t.astype(bf16)
    after = jnp.minimum(me + 1, cols - 1)

    loads[2].wait()

    def turn_block(b, carry):
        at_ref[b] = a_ref[b].astype(f32).T.astype(bf16)
        return carry

    lax.fori_loop(0, blocks, turn_block, 0, unroll=4)
    loads[3].wait()
    bit = jnp.left_shift(1, lax.broadcasted_iota(i32, (8, 128), 0))

    def open_mask(s, carry):
        for pair in range(8):
            parts = []
            for w in (2 * pair, 2 * pair + 1):
                word = jnp.broadcast_to(w_ref[s, w : w + 1, :], (8, 128))
                parts.append(jnp.where((word & bit) != 0, 1.0, 0.0))
            m_ref[s, 16 * pair : 16 * pair + 16, :] = jnp.concatenate(parts, axis=0).astype(bf16)
        return carry

    lax.fori_loop(0, slots, open_mask, 0, unroll=2)
    to_scalars.wait()

    def product(r_ref):
        def first_half(k, carry):
            code = code_sm[0, k]
            item = jnp.minimum(code & 63, blocks - 1)
            s, u = jnp.minimum((code >> 6) & 127, slots - 1), jnp.minimum((code >> 13) & 31, cols)
            scores = jnp.dot(at_ref[item], r_ref[u], preferred_element_type=f32)
            t_ref[k] = scores.astype(bf16) * m_ref[s]
            return carry

        def second_half(k, carry):
            acc, last = carry
            code = code_sm[0, k]
            item, u = jnp.minimum(code & 63, blocks - 1), code >> 13
            part = jnp.dot(a_ref[item], t_ref[k], preferred_element_type=f32)
            acc = jnp.where(u == last, acc, 0.0) + part
            s_ref[k + 1] = acc
            return acc, u

        lax.fori_loop(0, slots, first_half, 0, unroll=UNROLL)
        lax.fori_loop(
            0, slots, second_half, (jnp.zeros(s_ref.shape[1:], f32), i32(-1)), unroll=UNROLL
        )

    def summed(u):
        return s_ref[jnp.minimum(code_sm[1, u] & 127, slots)]

    def graph(r_ref):
        own, following = r_ref[me], r_ref[after]
        here = here_degree * own.astype(f32)
        here = here - jnp.dot(own, sym_ref[...], preferred_element_type=f32)
        here = here - jnp.dot(following, et_ref[...], preferred_element_type=f32)
        there = there_degree * following.astype(f32)
        there = there - jnp.dot(own, e_ref[...], preferred_element_type=f32)
        return GRAPH * here, GRAPH * there

    def partial(r_ref, x_ref, y_ref, send, recv):
        here, there = graph(r_ref)
        form = jnp.zeros(here.shape, f32)
        copies = []
        for i, peer in peers():
            value = summed(peer) + jnp.where(peer == me + 1, there, 0.0)
            form = form + r_ref[peer].astype(f32) * value
            x_ref[pl.ds(peer, 1)] = value.astype(bf16)[None]
            copy = pltpu.make_async_remote_copy(
                src_ref=x_ref.at[peer],
                dst_ref=y_ref.at[me],
                send_sem=send.at[i],
                recv_sem=recv.at[me],
                device_id={"col": peer},
                device_id_type=pl.DeviceIdType.MESH,
            )
            copy.start()
            copies.append(copy)
        own = summed(me) + here
        form = form + r_ref[me].astype(f32) * own
        return own, form, copies

    def total(own, y_ref, recv):
        for i, peer in peers():
            pltpu.make_async_copy(y_ref.at[peer], y_ref.at[peer], recv.at[peer]).wait()
            own = own + y_ref[peer].astype(f32)
        return own

    def by_lane(x):
        return jnp.sum(x, axis=0, keepdims=True)

    sublane = lax.broadcasted_iota(i32, (8, 128), 0)

    def stack(*lines):
        out = jnp.zeros((8, 128), f32)
        for n, line in enumerate(lines):
            out = jnp.where(sublane == n, line, out)
        return out

    def share(p_ref, value, send, recv):
        p_ref[pl.ds(me, 1)] = value[None]
        copies = gather(p_ref, send, recv)
        for copy in copies:
            copy.start()
        return copies

    def over_lanes(x):
        return jnp.sum(x, axis=1, keepdims=True)

    arrive(r1_ref, g1_recv)
    product(r1_ref)
    own, form, sent2 = partial(r1_ref, x1_ref, y1_ref, x1_send, x1_recv)
    form = form + RIDGE * rhs * rhs
    sent3 = share(p1_ref, stack(by_lane(rhs * rhs), by_lane(form)), p1_send, p1_recv)
    arrive(p1_ref, p1_recv)
    line = jnp.sum(p1_ref[...], axis=0)
    norm_line, form_line = line[0:1, :], line[1:2, :]
    norm_row, form_row = over_lanes(norm_line), over_lanes(form_line)
    shift = jnp.where(norm_row > 0.0, form_row / jnp.where(norm_row > 0.0, norm_row, 1.0), 0.0)
    w = total(own, y1_ref, x1_recv) + RIDGE * rhs

    v = w - shift * rhs
    r2_ref[pl.ds(me, 1)] = v.astype(bf16)[None]
    sent4 = gather(r2_ref, g2_send, g2_recv)
    for copy in sent4:
        copy.start()
    square = by_lane(w * w)
    arrive(r2_ref, g2_recv)
    product(r2_ref)
    own, form, sent5 = partial(r2_ref, x2_ref, y2_ref, x2_send, x2_recv)
    form = form + RIDGE * v * v
    sent6 = share(p2_ref, stack(square, by_lane(form)), p2_send, p2_recv)
    arrive(p2_ref, p2_recv)
    line = jnp.sum(p2_ref[...], axis=0)
    square_line, bent_line = line[0:1, :], line[1:2, :]
    cubic_line = bent_line + 2.0 * shift * square_line - shift * shift * form_line
    p3_ref[pl.ds(my_row, 1)] = stack(norm_line, form_line, square_line, cubic_line)[None]
    sent7 = []
    for o in range(1, rows):
        copy = pltpu.make_async_remote_copy(
            src_ref=p3_ref.at[my_row],
            dst_ref=p3_ref.at[my_row],
            send_sem=p3_send.at[o - 1],
            recv_sem=p3_recv.at[my_row],
            device_id={"row": lax.rem(my_row + o, rows)},
            device_id_type=pl.DeviceIdType.MESH,
        )
        copy.start()
        sent7.append(copy)
    hv = total(own, y2_ref, x2_recv) + RIDGE * v
    z = hv + shift * w
    for o in range(1, rows):
        other = lax.rem(my_row + o, rows)
        pltpu.make_async_copy(p3_ref.at[other], p3_ref.at[other], p3_recv.at[other]).wait()
    sums = over_lanes(jnp.sum(p3_ref[...], axis=0))
    norm0, form1, square1, cubic1 = (sums[n : n + 1, :] for n in range(4))
    alpha1 = norm0 / form1
    norm1 = norm0 - 2.0 * alpha1 * form1 + alpha1 * alpha1 * square1
    more = 1.0 + norm1 / norm0
    curve = more * more * form1 - 2.0 * more * alpha1 * square1 + alpha1 * alpha1 * cubic1
    alpha2 = norm1 / curve
    direction = more * rhs - alpha1 * w
    image = more * w - alpha1 * z
    sol_ref[0] = alpha1 * rhs + alpha2 * direction
    res_ref[0] = rhs - alpha1 * w - alpha2 * image

    for copies in (sent1, sent2, sent3, sent4, sent5, sent6, sent7):
        for copy in copies:
            copy.wait_send()


def per_device(rows, cols, *args):
    rhs, items, users, slot_items, counts, words, selfs, nexts = args
    slots = users.shape[2]
    blocks, rank, width = items.shape
    vmem = pl.BlockSpec(memory_space=pltpu.VMEM)
    smem = pl.BlockSpec(memory_space=pltpu.SMEM)
    hbm = pl.BlockSpec(memory_space=pl.ANY)
    dma = pltpu.SemaphoreType.DMA
    pair = [dma((cols - 1,)), dma((cols,))]
    block16 = (cols, rank, width)
    return pl.pallas_call(
        functools.partial(kernel, rows, cols),
        out_shape=[jax.ShapeDtypeStruct(rhs.shape, f32)] * 2,
        in_specs=[vmem, hbm, vmem, vmem, smem, hbm, hbm, hbm],
        out_specs=[vmem, vmem],
        scratch_shapes=[
            pltpu.VMEM((blocks, rank, width), bf16),
            pltpu.VMEM((blocks, width, rank), bf16),
            pltpu.VMEM((slots, width // 8, width), i32),
            pltpu.VMEM((slots, width, width), bf16),
            pltpu.VMEM((slots, width, width), bf16),
            pltpu.VMEM((slots + 1, rank, width), f32),
            pltpu.VMEM((cols + 1, rank, width), bf16),
            pltpu.VMEM((cols + 1, rank, width), bf16),
            pltpu.VMEM(block16, bf16),
            pltpu.VMEM(block16, bf16),
            pltpu.VMEM(block16, bf16),
            pltpu.VMEM(block16, bf16),
            pltpu.VMEM((width, width), i32),
            pltpu.VMEM((width, width), i32),
            pltpu.VMEM((width, width), bf16),
            pltpu.VMEM((width, width), bf16),
            pltpu.VMEM((width, width), bf16),
            pltpu.VMEM((8, 128), i32),
            pltpu.SMEM((8, 128), i32),
            pltpu.VMEM((cols, 8, 128), f32),
            pltpu.VMEM((cols, 8, 128), f32),
            pltpu.VMEM((rows, 8, 128), f32),
            dma((5,)),
            *pair * 6,
            dma((rows - 1,)),
            dma((rows,)),
        ],
        compiler_params=pltpu.CompilerParams(collective_id=0, has_side_effects=True),
        name="cg",
    )(*args)


def solution(mesh):
    rows, cols = mesh.shape["row"], mesh.shape["col"]
    user_blocks = P(("row", "col"), None, None)
    return jax.shard_map(
        functools.partial(per_device, rows, cols),
        mesh=mesh,
        in_specs=(
            user_blocks,
            P("col", None, None),
            P("row", "col", None),
            P("row", "col", None),
            P("row", "col"),
            P("row", "col", None, None, None),
            user_blocks,
            user_blocks,
        ),
        out_specs=(user_blocks, user_blocks),
        check_vma=False,
    )
```

```python
import functools

import jax
import jax.numpy as jnp
from jax import lax
from jax.experimental import pallas as pl
from jax.experimental.pallas import tpu as pltpu
from jax.sharding import PartitionSpec as P

GRAPH = 0.01
RIDGE = 0.5
UNROLL = 8
f32, bf16, i32 = jnp.float32, jnp.bfloat16, jnp.int32


def far_first(chips):
    return sorted(range(1, chips), key=lambda o: -min(o, chips - o))


def kernel(
    rows,
    cols,
    rhs_hbm,
    items_hbm,
    users_hbm,
    slot_items_hbm,
    count_hbm,
    words_hbm,
    self_hbm,
    next_hbm,
    out_ref,
    rhs_ref,
    users_ref,
    slot_items_ref,
    count_ref,
    a_ref,
    at_ref,
    w_ref,
    m_ref,
    t_ref,
    s_ref,
    r1_ref,
    r2_ref,
    x1_ref,
    x2_ref,
    yp1_ref,
    yp2_ref,
    z1_ref,
    z2_ref,
    y1_ref,
    y2_ref,
    self_ref,
    next_ref,
    sym_ref,
    e_ref,
    et_ref,
    code_ref,
    code_sm,
    p1_ref,
    p2_ref,
    p3_ref,
    local_sem,
    g1_send,
    g1_recv,
    g2_send,
    g2_recv,
    p1_send,
    p1_recv,
    p2_send,
    p2_recv,
    xp1_send,
    xp1_recv,
    xp2_send,
    xp2_recv,
    z1_send,
    z1_recv,
    z2_send,
    z2_recv,
    p3_send,
    p3_recv,
):
    slots = w_ref.shape[0]
    blocks = a_ref.shape[0]
    chips = cols // 2
    me = lax.axis_index("col")
    my_row = lax.axis_index("row")
    my_chip, my_core = me // 2, me % 2
    partner = my_chip * 2 + 1 - my_core
    far = far_first(chips)
    near = far[::-1]

    def chip(o):
        return lax.rem(my_chip + o, chips)

    def remote(src, dst, send, recv, where):
        copy = pltpu.make_async_remote_copy(
            src_ref=src,
            dst_ref=dst,
            send_sem=send,
            recv_sem=recv,
            device_id=where,
            device_id_type=pl.DeviceIdType.MESH,
        )
        copy.start()
        return copy

    def arrived(ref, sem):
        pltpu.make_async_copy(ref, ref, sem).wait()

    rhs_load = pltpu.make_async_copy(rhs_hbm.at[0], rhs_ref, local_sem.at[5])
    rhs_load.start()
    barrier = pltpu.get_barrier_semaphore()
    for o in range(1, rows):
        pl.semaphore_signal(
            barrier,
            inc=1,
            device_id={"row": lax.rem(my_row + o, rows)},
            device_id_type=pl.DeviceIdType.MESH,
        )
    for o in range(1, cols):
        pl.semaphore_signal(
            barrier,
            inc=1,
            device_id={"col": lax.rem(me + o, cols)},
            device_id_type=pl.DeviceIdType.MESH,
        )
    loads = [
        pltpu.make_async_copy(users_hbm.at[0], users_ref, local_sem.at[6]),
        pltpu.make_async_copy(slot_items_hbm.at[0], slot_items_ref, local_sem.at[7]),
        pltpu.make_async_copy(count_hbm, count_ref, local_sem.at[8]),
        pltpu.make_async_copy(self_hbm.at[0], self_ref, local_sem.at[0]),
        pltpu.make_async_copy(next_hbm.at[0], next_ref, local_sem.at[1]),
        pltpu.make_async_copy(items_hbm, a_ref, local_sem.at[2]),
        pltpu.make_async_copy(words_hbm.at[0, 0], w_ref, local_sem.at[3]),
    ]
    for load in loads:
        load.start()

    rhs_load.wait()
    rhs = rhs_ref[...]
    r1_ref[pl.ds(me, 1)] = rhs.astype(bf16)[None]
    r1_ref[cols] = jnp.zeros(r1_ref.shape[1:], bf16)
    r2_ref[cols] = jnp.zeros(r2_ref.shape[1:], bf16)
    s_ref[0] = jnp.zeros(s_ref.shape[1:], f32)

    pl.semaphore_wait(barrier, cols - 1 + rows - 1)

    def gather(r_ref, send, recv):
        copies = [
            remote(r_ref.at[me], r_ref.at[me], send.at[n], recv.at[me], {"col": chip(o) * 2 + my_core})
            for n, o in enumerate(far)
        ]
        n = chips - 1
        copies.append(remote(r_ref.at[me], r_ref.at[me], send.at[n], recv.at[me], {"col": partner}))
        return copies

    def pass_on(n, r_ref, send, recv):
        block = chip(near[n]) * 2 + my_core
        arrived(r_ref.at[block], recv.at[block])
        return remote(
            r_ref.at[block], r_ref.at[block], send.at[chips + n], recv.at[block], {"col": partner}
        )

    def finish(r_ref, recv):
        arrived(r_ref.at[partner], recv.at[partner])
        for o in near:
            block = chip(o) * 2 + 1 - my_core
            arrived(r_ref.at[block], recv.at[block])

    sent = gather(r1_ref, g1_send, g1_recv)

    for load in loads[:3]:
        load.wait()
    lane = lax.broadcasted_iota(i32, (1, 128), 1)
    code_ref[...] = jnp.broadcast_to((cols + 1) * 8192 + lane * 64, (8, 128))
    slot = lax.broadcasted_iota(i32, (1, slots), 1)
    user = jnp.where(slot < count_ref[...], users_ref[...], cols)
    code_ref[0:1, 0:slots] = user * 8192 + slot * 64 + slot_items_ref[...]
    across = jnp.broadcast_to(code_ref[0:1, :].astype(f32), (128, 128))
    down = across.T
    rank = jnp.sum(jnp.where(across < down, 1.0, 0.0), axis=1, keepdims=True)
    lanes = lax.broadcasted_iota(i32, (128, 128), 1).astype(f32)
    ordered = jnp.sum(jnp.where(rank == lanes, down, 0.0), axis=0, keepdims=True)
    upto = jnp.sum(jnp.where(down < (lanes + 1.0) * 8192.0, 1.0, 0.0), axis=0, keepdims=True)
    before = jnp.sum(jnp.where(down < lanes * 8192.0, 1.0, 0.0), axis=0, keepdims=True)
    code_ref[0:1, :] = ordered.astype(i32)
    code_ref[1:2, :] = jnp.where(upto > before, upto, 0.0).astype(i32)
    to_scalars = pltpu.make_async_copy(code_ref, code_sm, local_sem.at[4])
    to_scalars.start()

    loads[3].wait()
    loads[4].wait()
    first = self_ref[...].astype(f32)
    sym = first + first.T
    keep = jnp.where(me < cols - 1, 1.0, 0.0)
    edges = next_ref[...].astype(f32) * keep
    edges_t = edges.T
    there_degree = jnp.sum(edges, axis=0, keepdims=True)
    here_degree = jnp.sum(sym, axis=0, keepdims=True) + jnp.sum(edges_t, axis=0, keepdims=True)
    sym_ref[...] = sym.astype(bf16)
    e_ref[...] = edges.astype(bf16)
    et_ref[...] = edges_t.astype(bf16)
    after = jnp.minimum(me + 1, cols - 1)

    loads[5].wait()

    def turn_block(b, carry):
        at_ref[b] = a_ref[b].astype(f32).T.astype(bf16)
        return carry

    lax.fori_loop(0, blocks, turn_block, 0, unroll=4)
    loads[6].wait()
    bit = jnp.left_shift(1, lax.broadcasted_iota(i32, (8, 128), 0))

    def open_mask(s, carry):
        for pair in range(8):
            parts = []
            for w in (2 * pair, 2 * pair + 1):
                word = jnp.broadcast_to(w_ref[s, w : w + 1, :], (8, 128))
                parts.append(jnp.where((word & bit) != 0, 1.0, 0.0))
            m_ref[s, 16 * pair : 16 * pair + 16, :] = jnp.concatenate(parts, axis=0).astype(bf16)
        return carry

    cuts = [slots * n // (chips - 1) for n in range(chips)]
    for n in range(chips - 1):
        lax.fori_loop(cuts[n], cuts[n + 1], open_mask, 0, unroll=2)
        sent.append(pass_on(n, r1_ref, g1_send, g1_recv))
    to_scalars.wait()

    def by_lane(x):
        return jnp.sum(x, axis=0, keepdims=True)

    def over_lanes(x):
        return jnp.sum(x, axis=1, keepdims=True)

    sublane = lax.broadcasted_iota(i32, (8, 128), 0)

    def stack(*lines):
        out = jnp.zeros((8, 128), f32)
        for n, line in enumerate(lines):
            out = jnp.where(sublane == n, line, out)
        return out

    def first_half(r_ref):
        def turn(k, squares):
            code = code_sm[0, k]
            item = jnp.minimum(code & 63, blocks - 1)
            s, u = jnp.minimum((code >> 6) & 127, slots - 1), jnp.minimum((code >> 13) & 31, cols)
            scores = jnp.dot(at_ref[item], r_ref[u], preferred_element_type=f32)
            tile = scores.astype(bf16) * m_ref[s]
            t_ref[k] = tile
            square = scores * tile.astype(f32)
            return squares + jnp.sum(square.reshape(-1, 8, 128), axis=0)

        return lax.fori_loop(0, slots, turn, jnp.zeros((8, 128), f32), unroll=UNROLL)

    def second_half():
        def turn(k, carry):
            acc, last = carry
            code = code_sm[0, k]
            item, u = jnp.minimum(code & 63, blocks - 1), code >> 13
            part = jnp.dot(a_ref[item], t_ref[k], preferred_element_type=f32)
            acc = jnp.where(u == last, acc, 0.0) + part
            s_ref[k + 1] = acc
            return acc, u

        start = (jnp.zeros(s_ref.shape[1:], f32), i32(-1))
        lax.fori_loop(0, slots, turn, start, unroll=UNROLL)

    def summed(u):
        return s_ref[jnp.minimum(code_sm[1, u] & 127, slots)]

    def graph(r_ref):
        own, following = r_ref[me], r_ref[after]
        here = here_degree * own.astype(f32)
        here = here - jnp.dot(own, sym_ref[...], preferred_element_type=f32)
        here = here - jnp.dot(following, et_ref[...], preferred_element_type=f32)
        there = there_degree * following.astype(f32)
        there = there - jnp.dot(own, e_ref[...], preferred_element_type=f32)
        form = own.astype(f32) * here + following.astype(f32) * there
        return GRAPH * here, GRAPH * there, GRAPH * by_lane(form)

    def scatter(here, there, x_ref, yp_ref, z_ref, y_ref, xp_send, xp_recv, z_send, z_recv):
        copies = []
        for n, o in enumerate(far + [0]):
            p = chip(o)
            block = p * 2 + 1 - my_core
            value = summed(block) + jnp.where(block == me + 1, there, 0.0)
            x_ref[pl.ds(p, 1)] = value.astype(bf16)[None]
            copies.append(
                remote(x_ref.at[p], yp_ref.at[p], xp_send.at[n], xp_recv.at[p], {"col": partner})
            )
        for n, o in enumerate(far):
            p = chip(o)
            value = summed(p * 2 + my_core)
            arrived(yp_ref.at[p], xp_recv.at[p])
            z_ref[pl.ds(p, 1)] = (value + yp_ref[p].astype(f32)).astype(bf16)[None]
            copies.append(
                remote(
                    z_ref.at[p],
                    y_ref.at[my_chip],
                    z_send.at[n],
                    z_recv.at[my_chip],
                    {"col": p * 2 + my_core},
                )
            )
        arrived(yp_ref.at[my_chip], xp_recv.at[my_chip])
        return summed(me) + here + yp_ref[my_chip].astype(f32), copies

    def total(own, y_ref, z_recv):
        for o in near:
            p = chip(o)
            arrived(y_ref.at[p], z_recv.at[p])
            own = own + y_ref[p].astype(f32)
        return own

    def share(p_ref, value, send, recv):
        p_ref[pl.ds(me, 1)] = value[None]
        return [
            remote(
                p_ref.at[me],
                p_ref.at[me],
                send.at[o],
                recv.at[me],
                {"col": lax.rem(me + o, cols)},
            )
            for o in sorted(range(1, cols), key=lambda o: -min(o, cols - o))
        ]

    def all_shares(p_ref, recv):
        for o in range(1, cols):
            other = lax.rem(me + o, cols)
            arrived(p_ref.at[other], recv.at[other])
        return jnp.sum(p_ref[...], axis=0)

    finish(r1_ref, g1_recv)
    here, there, form = graph(r1_ref)
    form = form + by_lane(first_half(r1_ref)) + RIDGE * by_lane(rhs * rhs)
    sent += share(p1_ref, stack(by_lane(rhs * rhs), form), p1_send, p1_recv)
    second_half()
    own, copies = scatter(
        here, there, x1_ref, yp1_ref, z1_ref, y1_ref, xp1_send, xp1_recv, z1_send, z1_recv
    )
    sent += copies
    line = all_shares(p1_ref, p1_recv)
    norm_line, form_line = line[0:1, :], line[1:2, :]
    norm_row, form_row = over_lanes(norm_line), over_lanes(form_line)
    shift = jnp.where(norm_row > 0.0, form_row / jnp.where(norm_row > 0.0, norm_row, 1.0), 0.0)
    w = total(own, y1_ref, z1_recv) + RIDGE * rhs

    v = w - shift * rhs
    r2_ref[pl.ds(me, 1)] = v.astype(bf16)[None]
    sent += gather(r2_ref, g2_send, g2_recv)
    square = by_lane(w * w)
    for n in range(chips - 1):
        sent.append(pass_on(n, r2_ref, g2_send, g2_recv))
    finish(r2_ref, g2_recv)
    here, there, form = graph(r2_ref)
    form = form + by_lane(first_half(r2_ref)) + RIDGE * by_lane(v * v)
    sent += share(p2_ref, stack(square, form), p2_send, p2_recv)
    second_half()
    own, copies = scatter(
        here, there, x2_ref, yp2_ref, z2_ref, y2_ref, xp2_send, xp2_recv, z2_send, z2_recv
    )
    sent += copies
    line = all_shares(p2_ref, p2_recv)
    square_line, bent_line = line[0:1, :], line[1:2, :]
    cubic_line = bent_line + 2.0 * shift * square_line - shift * shift * form_line
    p3_ref[pl.ds(my_row, 1)] = stack(norm_line, form_line, square_line, cubic_line)[None]
    for o in range(1, rows):
        sent.append(
            remote(
                p3_ref.at[my_row],
                p3_ref.at[my_row],
                p3_send.at[o - 1],
                p3_recv.at[my_row],
                {"row": lax.rem(my_row + o, rows)},
            )
        )
    hv = total(own, y2_ref, z2_recv) + RIDGE * v
    z = hv + shift * w
    for o in range(1, rows):
        other = lax.rem(my_row + o, rows)
        arrived(p3_ref.at[other], p3_recv.at[other])
    sums = over_lanes(jnp.sum(p3_ref[...], axis=0))
    norm0, form1, square1, cubic1 = (sums[n : n + 1, :] for n in range(4))
    alpha1 = norm0 / form1
    norm1 = norm0 - 2.0 * alpha1 * form1 + alpha1 * alpha1 * square1
    more = 1.0 + norm1 / norm0
    curve = more * more * form1 - 2.0 * more * alpha1 * square1 + alpha1 * alpha1 * cubic1
    alpha2 = norm1 / curve
    plus, cross = alpha1 + alpha2 * more, alpha1 * alpha2
    out_ref[0] = (plus - 1.0) * rhs - cross * w
    out_ref[1] = cross * z - plus * w

    for copy in sent:
        copy.wait_send()


def per_device(rows, cols, *args):
    rhs, items, users, slot_items, counts, words, selfs, nexts = args
    slots = users.shape[2]
    blocks, rank, width = items.shape
    chips = cols // 2
    vmem = pl.BlockSpec(memory_space=pltpu.VMEM)
    hbm = pl.BlockSpec(memory_space=pl.ANY)
    dma = pltpu.SemaphoreType.DMA
    half = pltpu.VMEM((chips, rank, width), bf16)
    out = pl.pallas_call(
        functools.partial(kernel, rows, cols),
        out_shape=jax.ShapeDtypeStruct((2, rank, width), f32),
        in_specs=[hbm] * 8,
        out_specs=vmem,
        scratch_shapes=[
            pltpu.VMEM((rank, width), f32),
            pltpu.VMEM((1, slots), i32),
            pltpu.VMEM((1, slots), i32),
            pltpu.VMEM((1, 1), i32),
            pltpu.VMEM((blocks, rank, width), bf16),
            pltpu.VMEM((blocks, width, rank), bf16),
            pltpu.VMEM((slots, width // 8, width), i32),
            pltpu.VMEM((slots, width, width), bf16),
            pltpu.VMEM((slots, width, width), bf16),
            pltpu.VMEM((slots + 1, rank, width), f32),
            pltpu.VMEM((cols + 1, rank, width), bf16),
            pltpu.VMEM((cols + 1, rank, width), bf16),
            *[half] * 8,
            pltpu.VMEM((width, width), i32),
            pltpu.VMEM((width, width), i32),
            pltpu.VMEM((width, width), bf16),
            pltpu.VMEM((width, width), bf16),
            pltpu.VMEM((width, width), bf16),
            pltpu.VMEM((8, 128), i32),
            pltpu.SMEM((8, 128), i32),
            pltpu.VMEM((cols, 8, 128), f32),
            pltpu.VMEM((cols, 8, 128), f32),
            pltpu.VMEM((rows, 8, 128), f32),
            dma((9,)),
            *[dma((cols,))] * 8,
            *[dma((chips,))] * 8,
            dma((rows,)),
            dma((rows,)),
        ],
        compiler_params=pltpu.CompilerParams(collective_id=0, has_side_effects=True),
        name="cg",
    )(*args)
    return out[0:1] + rhs, out[1:2] + rhs


def solution(mesh):
    rows, cols = mesh.shape["row"], mesh.shape["col"]
    user_blocks = P(("row", "col"), None, None)
    return jax.shard_map(
        functools.partial(per_device, rows, cols),
        mesh=mesh,
        in_specs=(
            user_blocks,
            P("col", None, None),
            P("row", "col", None),
            P("row", "col", None),
            P("row", "col"),
            P("row", "col", None, None, None),
            user_blocks,
            user_blocks,
        ),
        out_specs=(user_blocks, user_blocks),
        check_vma=False,
    )
```

```python
import functools

import jax
import jax.numpy as jnp
from jax import lax
from jax.experimental import pallas as pl
from jax.experimental.pallas import tpu as pltpu
from jax.sharding import PartitionSpec as P

GRAPH = 0.01
RIDGE = 0.5
UNROLL = 16
f32, bf16, i32 = jnp.float32, jnp.bfloat16, jnp.int32


def far_first(chips):
    return sorted(range(1, chips), key=lambda o: -min(o, chips - o))


def kernel(
    rows,
    cols,
    rhs_hbm,
    items_hbm,
    users_hbm,
    slot_items_hbm,
    count_hbm,
    words_hbm,
    self_hbm,
    next_hbm,
    out_ref,
    rhs_ref,
    users_ref,
    slot_items_ref,
    count_ref,
    a_ref,
    at_ref,
    w_ref,
    m_ref,
    t_ref,
    s_ref,
    r1_ref,
    r2_ref,
    x1_ref,
    x2_ref,
    yp1_ref,
    yp2_ref,
    z1_ref,
    z2_ref,
    y1_ref,
    y2_ref,
    self_ref,
    next_ref,
    sym_ref,
    e_ref,
    et_ref,
    code_ref,
    code_sm,
    p1_ref,
    p2_ref,
    p3_ref,
    local_sem,
    g1_send,
    g1_recv,
    g2_send,
    g2_recv,
    p1_send,
    p1_recv,
    p2_send,
    p2_recv,
    xp1_send,
    xp1_recv,
    xp2_send,
    xp2_recv,
    z1_send,
    z1_recv,
    z2_send,
    z2_recv,
    p3_send,
    p3_recv,
):
    slots = w_ref.shape[0]
    blocks = a_ref.shape[0]
    chips = cols // 2
    me = lax.axis_index("col")
    my_row = lax.axis_index("row")
    my_chip, my_core = me // 2, me % 2
    partner = my_chip * 2 + 1 - my_core
    far = far_first(chips)
    near = far[::-1]

    def chip(o):
        return lax.rem(my_chip + o, chips)

    def remote(src, dst, send, recv, where):
        copy = pltpu.make_async_remote_copy(
            src_ref=src,
            dst_ref=dst,
            send_sem=send,
            recv_sem=recv,
            device_id=where,
            device_id_type=pl.DeviceIdType.MESH,
        )
        copy.start()
        return copy

    def arrived(ref, sem):
        pltpu.make_async_copy(ref, ref, sem).wait()

    rhs_load = pltpu.make_async_copy(rhs_hbm.at[0], rhs_ref, local_sem.at[5])
    rhs_load.start()
    barrier = pltpu.get_barrier_semaphore()
    for o in range(1, rows):
        pl.semaphore_signal(
            barrier,
            inc=1,
            device_id={"row": lax.rem(my_row + o, rows)},
            device_id_type=pl.DeviceIdType.MESH,
        )
    for o in range(1, cols):
        pl.semaphore_signal(
            barrier,
            inc=1,
            device_id={"col": lax.rem(me + o, cols)},
            device_id_type=pl.DeviceIdType.MESH,
        )
    loads = [
        pltpu.make_async_copy(users_hbm.at[0], users_ref, local_sem.at[6]),
        pltpu.make_async_copy(slot_items_hbm.at[0], slot_items_ref, local_sem.at[7]),
        pltpu.make_async_copy(count_hbm, count_ref, local_sem.at[8]),
        pltpu.make_async_copy(self_hbm.at[0], self_ref, local_sem.at[0]),
        pltpu.make_async_copy(next_hbm.at[0], next_ref, local_sem.at[1]),
        pltpu.make_async_copy(items_hbm, a_ref, local_sem.at[2]),
        pltpu.make_async_copy(words_hbm.at[0, 0], w_ref, local_sem.at[3]),
    ]
    for load in loads:
        load.start()

    rhs_load.wait()
    rhs = rhs_ref[...]
    r1_ref[pl.ds(me, 1)] = rhs.astype(bf16)[None]
    r1_ref[cols] = jnp.zeros(r1_ref.shape[1:], bf16)
    r2_ref[cols] = jnp.zeros(r2_ref.shape[1:], bf16)
    s_ref[0] = jnp.zeros(s_ref.shape[1:], f32)

    pl.semaphore_wait(barrier, cols - 1 + rows - 1)

    def gather(r_ref, send, recv):
        copies = [
            remote(r_ref.at[me], r_ref.at[me], send.at[n], recv.at[me], {"col": chip(o) * 2 + my_core})
            for n, o in enumerate(far)
        ]
        n = chips - 1
        copies.append(remote(r_ref.at[me], r_ref.at[me], send.at[n], recv.at[me], {"col": partner}))
        return copies

    def pass_on(n, r_ref, send, recv):
        block = chip(near[n]) * 2 + my_core
        arrived(r_ref.at[block], recv.at[block])
        return remote(
            r_ref.at[block], r_ref.at[block], send.at[chips + n], recv.at[block], {"col": partner}
        )

    def finish(r_ref, recv):
        arrived(r_ref.at[partner], recv.at[partner])
        for o in near:
            block = chip(o) * 2 + 1 - my_core
            arrived(r_ref.at[block], recv.at[block])

    sent = gather(r1_ref, g1_send, g1_recv)

    for load in loads[:3]:
        load.wait()
    lane = lax.broadcasted_iota(i32, (1, 128), 1)
    code_ref[...] = jnp.broadcast_to((cols + 1) * 8192 + lane * 64, (8, 128))
    slot = lax.broadcasted_iota(i32, (1, slots), 1)
    user = jnp.where(slot < count_ref[...], users_ref[...], cols)
    code_ref[0:1, 0:slots] = user * 8192 + slot * 64 + slot_items_ref[...]
    across = jnp.broadcast_to(code_ref[0:1, :].astype(f32), (128, 128))
    down = across.T
    rank = jnp.sum(jnp.where(across < down, 1.0, 0.0), axis=1, keepdims=True)
    lanes = lax.broadcasted_iota(i32, (128, 128), 1).astype(f32)
    ordered = jnp.sum(jnp.where(rank == lanes, down, 0.0), axis=0, keepdims=True)
    upto = jnp.sum(jnp.where(down < (lanes + 1.0) * 8192.0, 1.0, 0.0), axis=0, keepdims=True)
    before = jnp.sum(jnp.where(down < lanes * 8192.0, 1.0, 0.0), axis=0, keepdims=True)
    code_ref[0:1, :] = ordered.astype(i32)
    code_ref[1:2, :] = jnp.where(upto > before, upto, 0.0).astype(i32)
    to_scalars = pltpu.make_async_copy(code_ref, code_sm, local_sem.at[4])
    to_scalars.start()

    loads[3].wait()
    loads[4].wait()
    first = self_ref[...].astype(f32)
    sym = first + first.T
    keep = jnp.where(me < cols - 1, 1.0, 0.0)
    edges = next_ref[...].astype(f32) * keep
    edges_t = edges.T
    there_degree = jnp.sum(edges, axis=0, keepdims=True)
    here_degree = jnp.sum(sym, axis=0, keepdims=True) + jnp.sum(edges_t, axis=0, keepdims=True)
    sym_ref[...] = sym.astype(bf16)
    e_ref[...] = edges.astype(bf16)
    et_ref[...] = edges_t.astype(bf16)
    after = jnp.minimum(me + 1, cols - 1)

    loads[5].wait()

    def turn_block(b, carry):
        at_ref[b] = a_ref[b].astype(f32).T.astype(bf16)
        return carry

    lax.fori_loop(0, blocks, turn_block, 0, unroll=4)
    loads[6].wait()
    bit = jnp.left_shift(1, lax.broadcasted_iota(i32, (8, 128), 0))

    def open_mask(s, carry):
        for pair in range(8):
            parts = []
            for w in (2 * pair, 2 * pair + 1):
                word = jnp.broadcast_to(w_ref[s, w : w + 1, :], (8, 128))
                parts.append(jnp.where((word & bit) != 0, 1.0, 0.0))
            m_ref[s, 16 * pair : 16 * pair + 16, :] = jnp.concatenate(parts, axis=0).astype(bf16)
        return carry

    cuts = [slots * n // (chips - 1) for n in range(chips)]
    for n in range(chips - 1):
        lax.fori_loop(cuts[n], cuts[n + 1], open_mask, 0, unroll=2)
        sent.append(pass_on(n, r1_ref, g1_send, g1_recv))
    to_scalars.wait()

    def by_lane(x):
        return jnp.sum(x, axis=0, keepdims=True)

    def over_lanes(x):
        return jnp.sum(x, axis=1, keepdims=True)

    def pack(a, b):
        return jnp.where(lane < 64, a + pltpu.roll(a, 64, 1), b + pltpu.roll(b, 64, 1))

    def unpack(line):
        return over_lanes(jnp.where(lane < 64, line, 0.0)), over_lanes(jnp.where(lane < 64, 0.0, line))

    def first_half(r_ref):
        def turn(k, squares):
            code = code_sm[0, k]
            item = jnp.minimum(code & 63, blocks - 1)
            s, u = jnp.minimum((code >> 6) & 127, slots - 1), jnp.minimum((code >> 13) & 31, cols)
            scores = jnp.dot(at_ref[item], r_ref[u], preferred_element_type=f32)
            tile = scores.astype(bf16) * m_ref[s]
            t_ref[k] = tile
            square = scores * tile.astype(f32)
            return squares + jnp.sum(square.reshape(-1, 8, 128), axis=0)

        return lax.fori_loop(0, slots, turn, jnp.zeros((8, 128), f32), unroll=UNROLL)

    def second_half():
        def turn(k, carry):
            acc, last = carry
            code = code_sm[0, k]
            item, u = jnp.minimum(code & 63, blocks - 1), code >> 13
            part = jnp.dot(a_ref[item], t_ref[k], preferred_element_type=f32)
            acc = jnp.where(u == last, acc, 0.0) + part
            s_ref[k + 1] = acc
            return acc, u

        start = (jnp.zeros(s_ref.shape[1:], f32), i32(-1))
        lax.fori_loop(0, slots, turn, start, unroll=UNROLL)

    def halves(r_ref):
        def turn(k, carry):
            acc, last = carry
            code = code_sm[0, k]
            item = jnp.minimum(code & 63, blocks - 1)
            s, u = jnp.minimum((code >> 6) & 127, slots - 1), jnp.minimum((code >> 13) & 31, cols)
            scores = jnp.dot(at_ref[item], r_ref[u], preferred_element_type=f32)
            tile = scores.astype(bf16) * m_ref[s]
            part = jnp.dot(a_ref[item], tile, preferred_element_type=f32)
            acc = jnp.where(u == last, acc, 0.0) + part
            s_ref[k + 1] = acc
            return acc, u

        start = (jnp.zeros(s_ref.shape[1:], f32), i32(-1))
        lax.fori_loop(0, slots, turn, start, unroll=UNROLL)

    def summed(u):
        return s_ref[jnp.minimum(code_sm[1, u] & 127, slots)]

    def graph(r_ref):
        own, following = r_ref[me], r_ref[after]
        here = here_degree * own.astype(f32)
        here = here - jnp.dot(own, sym_ref[...], preferred_element_type=f32)
        here = here - jnp.dot(following, et_ref[...], preferred_element_type=f32)
        there = there_degree * following.astype(f32)
        there = there - jnp.dot(own, e_ref[...], preferred_element_type=f32)
        form = own.astype(f32) * here + following.astype(f32) * there
        return GRAPH * here, GRAPH * there, GRAPH * by_lane(form)

    def scatter(here, there, meanwhile, x_ref, yp_ref, z_ref, y_ref, xp_send, xp_recv, z_send, z_recv):
        copies = []
        for n, o in enumerate(far + [0]):
            p = chip(o)
            block = p * 2 + 1 - my_core
            value = summed(block) + jnp.where(block == me + 1, there, 0.0)
            x_ref[pl.ds(p, 1)] = value.astype(bf16)[None]
            copies.append(
                remote(x_ref.at[p], yp_ref.at[p], xp_send.at[n], xp_recv.at[p], {"col": partner})
            )
        copies += meanwhile()
        for n, o in enumerate(far):
            p = chip(o)
            value = summed(p * 2 + my_core)
            arrived(yp_ref.at[p], xp_recv.at[p])
            z_ref[pl.ds(p, 1)] = (value + yp_ref[p].astype(f32)).astype(bf16)[None]
            copies.append(
                remote(
                    z_ref.at[p],
                    y_ref.at[my_chip],
                    z_send.at[n],
                    z_recv.at[my_chip],
                    {"col": p * 2 + my_core},
                )
            )
        arrived(yp_ref.at[my_chip], xp_recv.at[my_chip])
        return summed(me) + here + yp_ref[my_chip].astype(f32), copies

    def total(own, y_ref, z_recv):
        for o in near:
            p = chip(o)
            arrived(y_ref.at[p], z_recv.at[p])
            own = own + y_ref[p].astype(f32)
        return own

    def share(p_ref, value, send, recv):
        p_ref[pl.ds(me, 1)] = value[None]
        return [
            remote(
                p_ref.at[me],
                p_ref.at[me],
                send.at[o],
                recv.at[me],
                {"col": lax.rem(me + o, cols)},
            )
            for o in sorted(range(1, cols), key=lambda o: -min(o, cols - o))
        ]

    def all_shares(p_ref, recv):
        for o in range(1, cols):
            other = lax.rem(me + o, cols)
            arrived(p_ref.at[other], recv.at[other])
        return jnp.sum(p_ref[...], axis=0)

    finish(r1_ref, g1_recv)
    here, there, near_form = graph(r1_ref)
    halves(r1_ref)

    def meanwhile():
        norm = by_lane(rhs * rhs)
        form = jnp.zeros(rhs.shape, f32)
        for u in range(cols):
            form = form + r1_ref[u].astype(f32) * summed(u)
        form = by_lane(form) + near_form + RIDGE * norm
        return share(p1_ref, pack(norm, form), p1_send, p1_recv)

    own, copies = scatter(
        here, there, meanwhile, x1_ref, yp1_ref, z1_ref, y1_ref, xp1_send, xp1_recv, z1_send, z1_recv
    )
    sent += copies
    norm_row, form_row = unpack(all_shares(p1_ref, p1_recv))
    shift = jnp.where(norm_row > 0.0, form_row / jnp.where(norm_row > 0.0, norm_row, 1.0), 0.0)
    w = total(own, y1_ref, z1_recv) + RIDGE * rhs

    v = w - shift * rhs
    r2_ref[pl.ds(me, 1)] = v.astype(bf16)[None]
    sent += gather(r2_ref, g2_send, g2_recv)
    square = by_lane(w * w)
    for n in range(chips - 1):
        sent.append(pass_on(n, r2_ref, g2_send, g2_recv))
    finish(r2_ref, g2_recv)
    here, there, form = graph(r2_ref)
    form = form + by_lane(first_half(r2_ref)) + RIDGE * by_lane(v * v)
    sent += share(p2_ref, pack(square, form), p2_send, p2_recv)
    second_half()
    own, copies = scatter(
        here, there, list, x2_ref, yp2_ref, z2_ref, y2_ref, xp2_send, xp2_recv, z2_send, z2_recv
    )
    sent += copies
    square_row, bent_row = unpack(all_shares(p2_ref, p2_recv))
    cubic_row = bent_row + 2.0 * shift * square_row - shift * shift * form_row
    line = jnp.where(lane < 64, square_row, cubic_row)
    line = jnp.where(lane == 0, norm_row, jnp.where(lane == 1, form_row, line))
    p3_ref[pl.ds(my_row, 1)] = line[None]
    for o in range(1, rows):
        sent.append(
            remote(
                p3_ref.at[my_row],
                p3_ref.at[my_row],
                p3_send.at[o - 1],
                p3_recv.at[my_row],
                {"row": lax.rem(my_row + o, rows)},
            )
        )
    hv = total(own, y2_ref, z2_recv) + RIDGE * v
    z = hv + shift * w
    for o in range(1, rows):
        other = lax.rem(my_row + o, rows)
        arrived(p3_ref.at[other], p3_recv.at[other])
    line = jnp.sum(p3_ref[...], axis=0)
    norm0, form1, square1, cubic1 = (
        over_lanes(jnp.where(lane == n, line, 0.0)) for n in (0, 1, 2, 64)
    )
    alpha1 = norm0 / form1
    norm1 = norm0 - 2.0 * alpha1 * form1 + alpha1 * alpha1 * square1
    more = 1.0 + norm1 / norm0
    curve = more * more * form1 - 2.0 * more * alpha1 * square1 + alpha1 * alpha1 * cubic1
    alpha2 = norm1 / curve
    plus, cross = alpha1 + alpha2 * more, alpha1 * alpha2
    out_ref[0] = (plus - 1.0) * rhs - cross * w
    out_ref[1] = cross * z - plus * w

    for copy in sent:
        copy.wait_send()


def per_device(rows, cols, *args):
    rhs, items, users, slot_items, counts, words, selfs, nexts = args
    slots = users.shape[2]
    blocks, rank, width = items.shape
    chips = cols // 2
    vmem = pl.BlockSpec(memory_space=pltpu.VMEM)
    hbm = pl.BlockSpec(memory_space=pltpu.HBM)
    dma = pltpu.SemaphoreType.DMA
    half = pltpu.VMEM((chips, rank, width), bf16)
    out = pl.pallas_call(
        functools.partial(kernel, rows, cols),
        out_shape=jax.ShapeDtypeStruct((2, rank, width), f32),
        in_specs=[hbm] * 8,
        out_specs=vmem,
        scratch_shapes=[
            pltpu.VMEM((rank, width), f32),
            pltpu.VMEM((1, slots), i32),
            pltpu.VMEM((1, slots), i32),
            pltpu.VMEM((1, 1), i32),
            pltpu.VMEM((blocks, rank, width), bf16),
            pltpu.VMEM((blocks, width, rank), bf16),
            pltpu.VMEM((slots, width // 8, width), i32),
            pltpu.VMEM((slots, width, width), bf16),
            pltpu.VMEM((slots, width, width), bf16),
            pltpu.VMEM((slots + 1, rank, width), f32),
            pltpu.VMEM((cols + 1, rank, width), bf16),
            pltpu.VMEM((cols + 1, rank, width), bf16),
            *[half] * 8,
            pltpu.VMEM((width, width), i32),
            pltpu.VMEM((width, width), i32),
            pltpu.VMEM((width, width), bf16),
            pltpu.VMEM((width, width), bf16),
            pltpu.VMEM((width, width), bf16),
            pltpu.VMEM((8, 128), i32),
            pltpu.SMEM((8, 128), i32),
            pltpu.VMEM((cols, 1, 128), f32),
            pltpu.VMEM((cols, 1, 128), f32),
            pltpu.VMEM((rows, 1, 128), f32),
            dma((9,)),
            *[dma((cols,))] * 8,
            *[dma((chips,))] * 8,
            dma((rows,)),
            dma((rows,)),
        ],
        compiler_params=pltpu.CompilerParams(collective_id=0, has_side_effects=True),
        name="cg",
    )(*args)
    return out[0:1] + rhs, out[1:2] + rhs


def solution(mesh):
    rows, cols = mesh.shape["row"], mesh.shape["col"]
    user_blocks = P(("row", "col"), None, None)
    return jax.shard_map(
        functools.partial(per_device, rows, cols),
        mesh=mesh,
        in_specs=(
            user_blocks,
            P("col", None, None),
            P("row", "col", None),
            P("row", "col", None),
            P("row", "col"),
            P("row", "col", None, None, None),
            user_blocks,
            user_blocks,
        ),
        out_specs=(user_blocks, user_blocks),
        check_vma=False,
    )
```

```python
import functools

import jax
import jax.numpy as jnp
from jax import lax
from jax.experimental import pallas as pl
from jax.experimental.pallas import tpu as pltpu
from jax.sharding import PartitionSpec as P

GRAPH = 0.01
RIDGE = 0.5
UNROLL = 48
f32, bf16, i32 = jnp.float32, jnp.bfloat16, jnp.int32


def far_first(chips):
    return sorted(range(1, chips), key=lambda o: -min(o, chips - o))


def kernel(
    rows,
    cols,
    rhs_hbm,
    items_hbm,
    users_hbm,
    slot_items_hbm,
    count_hbm,
    words_hbm,
    self_hbm,
    next_hbm,
    out_ref,
    rhs_ref,
    users_ref,
    slot_items_ref,
    count_ref,
    a_ref,
    at_ref,
    w_ref,
    m_ref,
    t_ref,
    s_ref,
    r1_ref,
    r2_ref,
    x1_ref,
    x2_ref,
    yp1_ref,
    yp2_ref,
    z1_ref,
    z2_ref,
    y1_ref,
    y2_ref,
    self_ref,
    next_ref,
    sym_ref,
    e_ref,
    et_ref,
    code_ref,
    code_sm,
    p1_ref,
    p2_ref,
    p3_ref,
    local_sem,
    g1_send,
    g1_recv,
    g2_send,
    g2_recv,
    p1_send,
    p1_recv,
    p2_send,
    p2_recv,
    xp1_send,
    xp1_recv,
    xp2_send,
    xp2_recv,
    z1_send,
    z1_recv,
    z2_send,
    z2_recv,
    p3_send,
    p3_recv,
):
    slots = w_ref.shape[0]
    blocks = a_ref.shape[0]
    chips = cols // 2
    me = lax.axis_index("col")
    my_row = lax.axis_index("row")
    my_chip, my_core = me // 2, me % 2
    partner = my_chip * 2 + 1 - my_core
    far = far_first(chips)
    near = far[::-1]

    def chip(o):
        return lax.rem(my_chip + o, chips)

    def remote(src, dst, send, recv, where):
        copy = pltpu.make_async_remote_copy(
            src_ref=src,
            dst_ref=dst,
            send_sem=send,
            recv_sem=recv,
            device_id=where,
            device_id_type=pl.DeviceIdType.MESH,
        )
        copy.start()
        return copy

    def arrived(ref, sem):
        pltpu.make_async_copy(ref, ref, sem).wait()

    rhs_load = pltpu.make_async_copy(rhs_hbm.at[0], rhs_ref, local_sem.at[5])
    rhs_load.start()
    barrier = pltpu.get_barrier_semaphore()
    for o in range(1, rows):
        pl.semaphore_signal(
            barrier,
            inc=1,
            device_id={"row": lax.rem(my_row + o, rows)},
            device_id_type=pl.DeviceIdType.MESH,
        )
    for o in range(1, cols):
        pl.semaphore_signal(
            barrier,
            inc=1,
            device_id={"col": lax.rem(me + o, cols)},
            device_id_type=pl.DeviceIdType.MESH,
        )
    loads = [
        pltpu.make_async_copy(users_hbm.at[0], users_ref, local_sem.at[6]),
        pltpu.make_async_copy(slot_items_hbm.at[0], slot_items_ref, local_sem.at[7]),
        pltpu.make_async_copy(count_hbm, count_ref, local_sem.at[8]),
        pltpu.make_async_copy(self_hbm.at[0], self_ref, local_sem.at[0]),
        pltpu.make_async_copy(next_hbm.at[0], next_ref, local_sem.at[1]),
        pltpu.make_async_copy(items_hbm, a_ref, local_sem.at[2]),
        pltpu.make_async_copy(words_hbm.at[0, 0], w_ref, local_sem.at[3]),
    ]
    for load in loads:
        load.start()

    rhs_load.wait()
    rhs = rhs_ref[...]
    r1_ref[pl.ds(me, 1)] = rhs.astype(bf16)[None]
    r1_ref[cols] = jnp.zeros(r1_ref.shape[1:], bf16)
    r2_ref[cols] = jnp.zeros(r2_ref.shape[1:], bf16)
    s_ref[0] = jnp.zeros(s_ref.shape[1:], f32)

    pl.semaphore_wait(barrier, cols - 1 + rows - 1)

    def gather(r_ref, send, recv):
        copies = [
            remote(r_ref.at[me], r_ref.at[me], send.at[n], recv.at[me], {"col": chip(o) * 2 + my_core})
            for n, o in enumerate(far)
        ]
        n = chips - 1
        copies.append(remote(r_ref.at[me], r_ref.at[me], send.at[n], recv.at[me], {"col": partner}))
        return copies

    def pass_on(n, r_ref, send, recv):
        block = chip(near[n]) * 2 + my_core
        arrived(r_ref.at[block], recv.at[block])
        return remote(
            r_ref.at[block], r_ref.at[block], send.at[chips + n], recv.at[block], {"col": partner}
        )

    def finish(r_ref, recv):
        arrived(r_ref.at[partner], recv.at[partner])
        for o in near:
            block = chip(o) * 2 + 1 - my_core
            arrived(r_ref.at[block], recv.at[block])

    sent = gather(r1_ref, g1_send, g1_recv)

    for load in loads[:3]:
        load.wait()
    lane = lax.broadcasted_iota(i32, (1, 128), 1)
    code_ref[...] = jnp.broadcast_to((cols + 1) * 8192 + lane * 64, (8, 128))
    slot = lax.broadcasted_iota(i32, (1, slots), 1)
    user = jnp.where(slot < count_ref[...], users_ref[...], cols)
    code_ref[0:1, 0:slots] = user * 8192 + slot * 64 + slot_items_ref[...]
    across = jnp.broadcast_to(code_ref[0:1, :].astype(f32), (128, 128))
    down = across.T
    rank = jnp.sum(jnp.where(across < down, 1.0, 0.0), axis=1, keepdims=True)
    lanes = lax.broadcasted_iota(i32, (128, 128), 1).astype(f32)
    ordered = jnp.sum(jnp.where(rank == lanes, down, 0.0), axis=0, keepdims=True)
    upto = jnp.sum(jnp.where(down < (lanes + 1.0) * 8192.0, 1.0, 0.0), axis=0, keepdims=True)
    before = jnp.sum(jnp.where(down < lanes * 8192.0, 1.0, 0.0), axis=0, keepdims=True)
    code_ref[0:1, :] = ordered.astype(i32)
    code_ref[1:2, :] = jnp.where(upto > before, upto, 0.0).astype(i32)
    to_scalars = pltpu.make_async_copy(code_ref, code_sm, local_sem.at[4])
    to_scalars.start()

    loads[3].wait()
    loads[4].wait()
    first = self_ref[...].astype(f32)
    sym = first + first.T
    keep = jnp.where(me < cols - 1, 1.0, 0.0)
    edges = next_ref[...].astype(f32) * keep
    edges_t = edges.T
    there_degree = jnp.sum(edges, axis=0, keepdims=True)
    here_degree = jnp.sum(sym, axis=0, keepdims=True) + jnp.sum(edges_t, axis=0, keepdims=True)
    sym_ref[...] = sym.astype(bf16)
    e_ref[...] = edges.astype(bf16)
    et_ref[...] = edges_t.astype(bf16)
    after = jnp.minimum(me + 1, cols - 1)

    loads[5].wait()

    def turn_block(b, carry):
        at_ref[b] = a_ref[b].astype(f32).T.astype(bf16)
        return carry

    lax.fori_loop(0, blocks, turn_block, 0, unroll=4)
    loads[6].wait()
    bit = jnp.left_shift(1, lax.broadcasted_iota(i32, (8, 128), 0))

    def open_mask(s, carry):
        for pair in range(8):
            parts = []
            for w in (2 * pair, 2 * pair + 1):
                word = jnp.broadcast_to(w_ref[s, w : w + 1, :], (8, 128))
                parts.append(jnp.where((word & bit) != 0, 1.0, 0.0))
            m_ref[s, 16 * pair : 16 * pair + 16, :] = jnp.concatenate(parts, axis=0).astype(bf16)
        return carry

    cuts = [slots * n // (chips - 1) for n in range(chips)]
    for n in range(chips - 1):
        lax.fori_loop(cuts[n], cuts[n + 1], open_mask, 0, unroll=2)
        sent.append(pass_on(n, r1_ref, g1_send, g1_recv))
    to_scalars.wait()

    def by_lane(x):
        return jnp.sum(x, axis=0, keepdims=True)

    def over_lanes(x):
        return jnp.sum(x, axis=1, keepdims=True)

    def pack(a, b):
        return jnp.where(lane < 64, a + pltpu.roll(a, 64, 1), b + pltpu.roll(b, 64, 1))

    def unpack(line):
        return over_lanes(jnp.where(lane < 64, line, 0.0)), over_lanes(jnp.where(lane < 64, 0.0, line))

    def first_half(r_ref):
        def turn(k, squares):
            code = code_sm[0, k]
            item = jnp.minimum(code & 63, blocks - 1)
            s, u = jnp.minimum((code >> 6) & 127, slots - 1), jnp.minimum((code >> 13) & 31, cols)
            scores = jnp.dot(at_ref[item], r_ref[u], preferred_element_type=f32)
            tile = scores.astype(bf16) * m_ref[s]
            t_ref[k] = tile
            square = scores * tile.astype(f32)
            return squares + jnp.sum(square.reshape(-1, 8, 128), axis=0)

        return lax.fori_loop(0, slots, turn, jnp.zeros((8, 128), f32), unroll=UNROLL)

    def second_half():
        def turn(k, carry):
            acc, last = carry
            code = code_sm[0, k]
            item, u = jnp.minimum(code & 63, blocks - 1), code >> 13
            part = jnp.dot(a_ref[item], t_ref[k], preferred_element_type=f32)
            acc = jnp.where(u == last, acc, 0.0) + part
            s_ref[k + 1] = acc
            return acc, u

        start = (jnp.zeros(s_ref.shape[1:], f32), i32(-1))
        lax.fori_loop(0, slots, turn, start, unroll=UNROLL)

    def halves(r_ref):
        def turn(k, carry):
            acc, last = carry
            code = code_sm[0, k]
            item = jnp.minimum(code & 63, blocks - 1)
            s, u = jnp.minimum((code >> 6) & 127, slots - 1), jnp.minimum((code >> 13) & 31, cols)
            scores = jnp.dot(at_ref[item], r_ref[u], preferred_element_type=f32)
            tile = scores.astype(bf16) * m_ref[s]
            part = jnp.dot(a_ref[item], tile, preferred_element_type=f32)
            acc = jnp.where(u == last, acc, 0.0) + part
            s_ref[k + 1] = acc
            return acc, u

        start = (jnp.zeros(s_ref.shape[1:], f32), i32(-1))
        lax.fori_loop(0, slots, turn, start, unroll=UNROLL)

    def summed(u):
        return s_ref[jnp.minimum(code_sm[1, u] & 127, slots)]

    def graph(r_ref):
        own, following = r_ref[me], r_ref[after]
        here = here_degree * own.astype(f32)
        here = here - jnp.dot(own, sym_ref[...], preferred_element_type=f32)
        here = here - jnp.dot(following, et_ref[...], preferred_element_type=f32)
        there = there_degree * following.astype(f32)
        there = there - jnp.dot(own, e_ref[...], preferred_element_type=f32)
        form = own.astype(f32) * here + following.astype(f32) * there
        return GRAPH * here, GRAPH * there, GRAPH * by_lane(form)

    def scatter(here, there, meanwhile, x_ref, yp_ref, z_ref, y_ref, xp_send, xp_recv, z_send, z_recv):
        copies = []
        for n, o in enumerate(far + [0]):
            p = chip(o)
            block = p * 2 + 1 - my_core
            value = summed(block) + jnp.where(block == me + 1, there, 0.0)
            x_ref[pl.ds(p, 1)] = value.astype(bf16)[None]
            copies.append(
                remote(x_ref.at[p], yp_ref.at[p], xp_send.at[n], xp_recv.at[p], {"col": partner})
            )
        copies += meanwhile()
        for n, o in enumerate(far):
            p = chip(o)
            value = summed(p * 2 + my_core)
            arrived(yp_ref.at[p], xp_recv.at[p])
            z_ref[pl.ds(p, 1)] = (value + yp_ref[p].astype(f32)).astype(bf16)[None]
            copies.append(
                remote(
                    z_ref.at[p],
                    y_ref.at[my_chip],
                    z_send.at[n],
                    z_recv.at[my_chip],
                    {"col": p * 2 + my_core},
                )
            )
        arrived(yp_ref.at[my_chip], xp_recv.at[my_chip])
        return summed(me) + here + yp_ref[my_chip].astype(f32), copies

    def total(own, y_ref, z_recv):
        for o in near:
            p = chip(o)
            arrived(y_ref.at[p], z_recv.at[p])
            own = own + y_ref[p].astype(f32)
        return own

    def share(p_ref, value, send, recv):
        p_ref[pl.ds(me, 1)] = value[None]
        return [
            remote(
                p_ref.at[me],
                p_ref.at[me],
                send.at[o],
                recv.at[me],
                {"col": lax.rem(me + o, cols)},
            )
            for o in sorted(range(1, cols), key=lambda o: -min(o, cols - o))
        ]

    def all_shares(p_ref, recv):
        for o in range(1, cols):
            other = lax.rem(me + o, cols)
            arrived(p_ref.at[other], recv.at[other])
        return jnp.sum(p_ref[...], axis=0)

    finish(r1_ref, g1_recv)
    here, there, near_form = graph(r1_ref)
    halves(r1_ref)

    def meanwhile():
        norm = by_lane(rhs * rhs)
        form = jnp.zeros(rhs.shape, f32)
        for u in range(cols):
            form = form + r1_ref[u].astype(f32) * summed(u)
        form = by_lane(form) + near_form + RIDGE * norm
        return share(p1_ref, pack(norm, form), p1_send, p1_recv)

    own, copies = scatter(
        here, there, meanwhile, x1_ref, yp1_ref, z1_ref, y1_ref, xp1_send, xp1_recv, z1_send, z1_recv
    )
    sent += copies
    norm_row, form_row = unpack(all_shares(p1_ref, p1_recv))
    shift = jnp.where(norm_row > 0.0, form_row / jnp.where(norm_row > 0.0, norm_row, 1.0), 0.0)
    w = total(own, y1_ref, z1_recv) + RIDGE * rhs

    v = w - shift * rhs
    r2_ref[pl.ds(me, 1)] = v.astype(bf16)[None]
    sent += gather(r2_ref, g2_send, g2_recv)
    square = by_lane(w * w)
    for n in range(chips - 1):
        sent.append(pass_on(n, r2_ref, g2_send, g2_recv))
    finish(r2_ref, g2_recv)
    here, there, form = graph(r2_ref)
    form = form + by_lane(first_half(r2_ref)) + RIDGE * by_lane(v * v)
    sent += share(p2_ref, pack(square, form), p2_send, p2_recv)
    second_half()
    own, copies = scatter(
        here, there, list, x2_ref, yp2_ref, z2_ref, y2_ref, xp2_send, xp2_recv, z2_send, z2_recv
    )
    sent += copies
    square_row, bent_row = unpack(all_shares(p2_ref, p2_recv))
    cubic_row = bent_row + 2.0 * shift * square_row - shift * shift * form_row
    line = jnp.where(lane < 64, square_row, cubic_row)
    line = jnp.where(lane == 0, norm_row, jnp.where(lane == 1, form_row, line))
    p3_ref[pl.ds(my_row, 1)] = line[None]
    for o in range(1, rows):
        sent.append(
            remote(
                p3_ref.at[my_row],
                p3_ref.at[my_row],
                p3_send.at[o - 1],
                p3_recv.at[my_row],
                {"row": lax.rem(my_row + o, rows)},
            )
        )
    hv = total(own, y2_ref, z2_recv) + RIDGE * v
    z = hv + shift * w
    for o in range(1, rows):
        other = lax.rem(my_row + o, rows)
        arrived(p3_ref.at[other], p3_recv.at[other])
    line = jnp.sum(p3_ref[...], axis=0)
    norm0, form1, square1, cubic1 = (
        over_lanes(jnp.where(lane == n, line, 0.0)) for n in (0, 1, 2, 64)
    )
    alpha1 = norm0 / form1
    norm1 = norm0 - 2.0 * alpha1 * form1 + alpha1 * alpha1 * square1
    more = 1.0 + norm1 / norm0
    curve = more * more * form1 - 2.0 * more * alpha1 * square1 + alpha1 * alpha1 * cubic1
    alpha2 = norm1 / curve
    plus, cross = alpha1 + alpha2 * more, alpha1 * alpha2
    out_ref[0] = (plus - 1.0) * rhs - cross * w
    out_ref[1] = cross * z - plus * w

    for copy in sent:
        copy.wait_send()


def per_device(rows, cols, *args):
    rhs, items, users, slot_items, counts, words, selfs, nexts = args
    slots = users.shape[2]
    blocks, rank, width = items.shape
    chips = cols // 2
    vmem = pl.BlockSpec(memory_space=pltpu.VMEM)
    hbm = pl.BlockSpec(memory_space=pltpu.HBM)
    dma = pltpu.SemaphoreType.DMA
    half = pltpu.VMEM((chips, rank, width), bf16)
    out = pl.pallas_call(
        functools.partial(kernel, rows, cols),
        out_shape=jax.ShapeDtypeStruct((2, rank, width), f32),
        in_specs=[hbm] * 8,
        out_specs=vmem,
        scratch_shapes=[
            pltpu.VMEM((rank, width), f32),
            pltpu.VMEM((1, slots), i32),
            pltpu.VMEM((1, slots), i32),
            pltpu.VMEM((1, 1), i32),
            pltpu.VMEM((blocks, rank, width), bf16),
            pltpu.VMEM((blocks, width, rank), bf16),
            pltpu.VMEM((slots, width // 8, width), i32),
            pltpu.VMEM((slots, width, width), bf16),
            pltpu.VMEM((slots, width, width), bf16),
            pltpu.VMEM((slots + 1, rank, width), f32),
            pltpu.VMEM((cols + 1, rank, width), bf16),
            pltpu.VMEM((cols + 1, rank, width), bf16),
            *[half] * 8,
            pltpu.VMEM((width, width), i32),
            pltpu.VMEM((width, width), i32),
            pltpu.VMEM((width, width), bf16),
            pltpu.VMEM((width, width), bf16),
            pltpu.VMEM((width, width), bf16),
            pltpu.VMEM((8, 128), i32),
            pltpu.SMEM((8, 128), i32),
            pltpu.VMEM((cols, 1, 128), f32),
            pltpu.VMEM((cols, 1, 128), f32),
            pltpu.VMEM((rows, 1, 128), f32),
            dma((9,)),
            *[dma((cols,))] * 8,
            *[dma((chips,))] * 8,
            dma((rows,)),
            dma((rows,)),
        ],
        compiler_params=pltpu.CompilerParams(collective_id=0, has_side_effects=True),
        name="cg",
    )(*args)
    return out[0:1] + rhs, out[1:2] + rhs


def solution(mesh):
    rows, cols = mesh.shape["row"], mesh.shape["col"]
    user_blocks = P(("row", "col"), None, None)
    return jax.shard_map(
        functools.partial(per_device, rows, cols),
        mesh=mesh,
        in_specs=(
            user_blocks,
            P("col", None, None),
            P("row", "col", None),
            P("row", "col", None),
            P("row", "col"),
            P("row", "col", None, None, None),
            user_blocks,
            user_blocks,
        ),
        out_specs=(user_blocks, user_blocks),
        check_vma=False,
    )
```

```python
import functools

import jax
import jax.numpy as jnp
from jax import lax
from jax.experimental import pallas as pl
from jax.experimental.pallas import tpu as pltpu
from jax.sharding import PartitionSpec as P

GRAPH = 0.01
RIDGE = 0.5
UNROLL = 48
f32, bf16, i32 = jnp.float32, jnp.bfloat16, jnp.int32


def far_first(chips):
    return sorted(range(1, chips), key=lambda o: -min(o, chips - o))


def kernel(
    rows,
    cols,
    rhs_hbm,
    items_hbm,
    users_hbm,
    slot_items_hbm,
    count_hbm,
    words_hbm,
    self_hbm,
    next_hbm,
    out_ref,
    rhs_ref,
    users_ref,
    slot_items_ref,
    count_ref,
    a_ref,
    at_ref,
    w_ref,
    m_ref,
    t_ref,
    s_ref,
    r1_ref,
    r2_ref,
    x1_ref,
    x2_ref,
    yp1_ref,
    yp2_ref,
    z1_ref,
    z2_ref,
    y1_ref,
    y2_ref,
    self_ref,
    next_ref,
    sym_ref,
    e_ref,
    et_ref,
    code_ref,
    code_sm,
    p1_ref,
    p2_ref,
    p3_ref,
    local_sem,
    g1_send,
    g1_recv,
    g2_send,
    g2_recv,
    p1_send,
    p1_recv,
    p2_send,
    p2_recv,
    xp1_send,
    xp1_recv,
    xp2_send,
    xp2_recv,
    z1_send,
    z1_recv,
    z2_send,
    z2_recv,
    p3_send,
    p3_recv,
):
    slots = w_ref.shape[0]
    blocks = a_ref.shape[0]
    chips = cols // 2
    me = lax.axis_index("col")
    my_row = lax.axis_index("row")
    my_chip, my_core = me // 2, me % 2
    partner = my_chip * 2 + 1 - my_core
    far = far_first(chips)
    near = far[::-1]

    def chip(o):
        return lax.rem(my_chip + o, chips)

    def remote(src, dst, send, recv, where):
        copy = pltpu.make_async_remote_copy(
            src_ref=src,
            dst_ref=dst,
            send_sem=send,
            recv_sem=recv,
            device_id=where,
            device_id_type=pl.DeviceIdType.MESH,
        )
        copy.start()
        return copy

    def arrived(ref, sem):
        pltpu.make_async_copy(ref, ref, sem).wait()

    rhs_load = pltpu.make_async_copy(rhs_hbm.at[0], rhs_ref, local_sem.at[5])
    rhs_load.start()
    barrier = pltpu.get_barrier_semaphore()
    for o in range(1, rows):
        pl.semaphore_signal(
            barrier,
            inc=1,
            device_id={"row": lax.rem(my_row + o, rows)},
            device_id_type=pl.DeviceIdType.MESH,
        )
    for o in range(1, cols):
        pl.semaphore_signal(
            barrier,
            inc=1,
            device_id={"col": lax.rem(me + o, cols)},
            device_id_type=pl.DeviceIdType.MESH,
        )
    loads = [
        pltpu.make_async_copy(users_hbm.at[0], users_ref, local_sem.at[6]),
        pltpu.make_async_copy(slot_items_hbm.at[0], slot_items_ref, local_sem.at[7]),
        pltpu.make_async_copy(count_hbm, count_ref, local_sem.at[8]),
        pltpu.make_async_copy(self_hbm.at[0], self_ref, local_sem.at[0]),
        pltpu.make_async_copy(next_hbm.at[0], next_ref, local_sem.at[1]),
        pltpu.make_async_copy(items_hbm, a_ref, local_sem.at[2]),
        pltpu.make_async_copy(words_hbm.at[0, 0], w_ref, local_sem.at[3]),
    ]
    for load in loads:
        load.start()

    rhs_load.wait()
    rhs = rhs_ref[...]
    r1_ref[pl.ds(me, 1)] = rhs.astype(bf16)[None]
    r1_ref[cols] = jnp.zeros(r1_ref.shape[1:], bf16)
    r2_ref[cols] = jnp.zeros(r2_ref.shape[1:], bf16)
    s_ref[0] = jnp.zeros(s_ref.shape[1:], f32)

    pl.semaphore_wait(barrier, cols - 1 + rows - 1)

    def gather(r_ref, send, recv):
        copies = [
            remote(r_ref.at[me], r_ref.at[me], send.at[n], recv.at[me], {"col": chip(o) * 2 + my_core})
            for n, o in enumerate(far)
        ]
        n = chips - 1
        copies.append(remote(r_ref.at[me], r_ref.at[me], send.at[n], recv.at[me], {"col": partner}))
        return copies

    def pass_on(n, r_ref, send, recv):
        block = chip(near[n]) * 2 + my_core
        arrived(r_ref.at[block], recv.at[block])
        return remote(
            r_ref.at[block], r_ref.at[block], send.at[chips + n], recv.at[block], {"col": partner}
        )

    def finish(r_ref, recv):
        arrived(r_ref.at[partner], recv.at[partner])
        for o in near:
            block = chip(o) * 2 + 1 - my_core
            arrived(r_ref.at[block], recv.at[block])

    sent = gather(r1_ref, g1_send, g1_recv)

    for load in loads[:3]:
        load.wait()
    lane = lax.broadcasted_iota(i32, (1, 128), 1)
    code_ref[...] = jnp.broadcast_to((cols + 1) * 8192 + lane * 64, (8, 128))
    slot = lax.broadcasted_iota(i32, (1, slots), 1)
    user = jnp.where(slot < count_ref[...], users_ref[...], cols)
    code_ref[0:1, 0:slots] = user * 8192 + slot * 64 + slot_items_ref[...]
    across = jnp.broadcast_to(code_ref[0:1, :].astype(f32), (128, 128))
    down = across.T
    rank = jnp.sum(jnp.where(across < down, 1.0, 0.0), axis=1, keepdims=True)
    lanes = lax.broadcasted_iota(i32, (128, 128), 1).astype(f32)
    ordered = jnp.sum(jnp.where(rank == lanes, down, 0.0), axis=0, keepdims=True)
    upto = jnp.sum(jnp.where(down < (lanes + 1.0) * 8192.0, 1.0, 0.0), axis=0, keepdims=True)
    before = jnp.sum(jnp.where(down < lanes * 8192.0, 1.0, 0.0), axis=0, keepdims=True)
    code_ref[0:1, :] = ordered.astype(i32)
    code_ref[1:2, :] = jnp.where(upto > before, upto, 0.0).astype(i32)
    to_scalars = pltpu.make_async_copy(code_ref, code_sm, local_sem.at[4])
    to_scalars.start()

    loads[3].wait()
    loads[4].wait()
    first = self_ref[...].astype(f32)
    sym = first + first.T
    keep = jnp.where(me < cols - 1, 1.0, 0.0)
    edges = next_ref[...].astype(f32) * keep
    edges_t = edges.T
    there_degree = jnp.sum(edges, axis=0, keepdims=True)
    here_degree = jnp.sum(sym, axis=0, keepdims=True) + jnp.sum(edges_t, axis=0, keepdims=True)
    sym_ref[...] = sym.astype(bf16)
    e_ref[...] = edges.astype(bf16)
    et_ref[...] = edges_t.astype(bf16)
    after = jnp.minimum(me + 1, cols - 1)

    loads[5].wait()

    def turn_block(b, carry):
        at_ref[b] = a_ref[b].astype(f32).T.astype(bf16)
        return carry

    lax.fori_loop(0, blocks, turn_block, 0, unroll=4)
    loads[6].wait()
    bit = jnp.left_shift(1, lax.broadcasted_iota(i32, (8, 128), 0))

    def open_mask(s, carry):
        for pair in range(8):
            parts = []
            for w in (2 * pair, 2 * pair + 1):
                word = jnp.broadcast_to(w_ref[s, w : w + 1, :], (8, 128))
                parts.append(jnp.where((word & bit) != 0, 1.0, 0.0))
            m_ref[s, 16 * pair : 16 * pair + 16, :] = jnp.concatenate(parts, axis=0).astype(bf16)
        return carry

    cuts = [slots * n // (chips - 1) for n in range(chips)]
    for n in range(chips - 1):
        lax.fori_loop(cuts[n], cuts[n + 1], open_mask, 0, unroll=2)
        sent.append(pass_on(n, r1_ref, g1_send, g1_recv))
    to_scalars.wait()

    def by_lane(x):
        return jnp.sum(x, axis=0, keepdims=True)

    def over_lanes(x):
        return jnp.sum(x, axis=1, keepdims=True)

    def pack(a, b):
        return jnp.where(lane < 64, a + pltpu.roll(a, 64, 1), b + pltpu.roll(b, 64, 1))

    def unpack(line):
        return over_lanes(jnp.where(lane < 64, line, 0.0)), over_lanes(jnp.where(lane < 64, 0.0, line))

    def first_half(r_ref):
        def turn(k, squares):
            code = code_sm[0, k]
            item = jnp.minimum(code & 63, blocks - 1)
            s, u = jnp.minimum((code >> 6) & 127, slots - 1), jnp.minimum((code >> 13) & 31, cols)
            scores = jnp.dot(at_ref[item], r_ref[u], preferred_element_type=f32)
            tile = scores.astype(bf16) * m_ref[s]
            t_ref[k] = tile
            square = scores * tile.astype(f32)
            return squares + jnp.sum(square.reshape(-1, 8, 128), axis=0)

        return lax.fori_loop(0, slots, turn, jnp.zeros((8, 128), f32), unroll=UNROLL)

    def second_half():
        def turn(k, carry):
            acc, last = carry
            code = code_sm[0, k]
            item, u = jnp.minimum(code & 63, blocks - 1), code >> 13
            part = jnp.dot(a_ref[item], t_ref[k], preferred_element_type=f32)
            acc = jnp.where(u == last, acc, 0.0) + part
            s_ref[k + 1] = acc
            return acc, u

        start = (jnp.zeros(s_ref.shape[1:], f32), i32(-1))
        lax.fori_loop(0, slots, turn, start, unroll=UNROLL)

    def halves(r_ref):
        def turn(k, carry):
            acc, last = carry
            code = code_sm[0, k]
            item = jnp.minimum(code & 63, blocks - 1)
            s, u = jnp.minimum((code >> 6) & 127, slots - 1), jnp.minimum((code >> 13) & 31, cols)
            scores = jnp.dot(at_ref[item], r_ref[u], preferred_element_type=f32)
            tile = scores.astype(bf16) * m_ref[s]
            part = jnp.dot(a_ref[item], tile, preferred_element_type=f32)
            acc = jnp.where(u == last, acc, 0.0) + part
            s_ref[k + 1] = acc
            return acc, u

        start = (jnp.zeros(s_ref.shape[1:], f32), i32(-1))
        lax.fori_loop(0, slots, turn, start, unroll=UNROLL)

    def summed(u):
        return s_ref[jnp.minimum(code_sm[1, u] & 127, slots)]

    def graph(r_ref):
        own, following = r_ref[me], r_ref[after]
        here = here_degree * own.astype(f32)
        here = here - jnp.dot(own, sym_ref[...], preferred_element_type=f32)
        here = here - jnp.dot(following, et_ref[...], preferred_element_type=f32)
        there = there_degree * following.astype(f32)
        there = there - jnp.dot(own, e_ref[...], preferred_element_type=f32)
        form = own.astype(f32) * here + following.astype(f32) * there
        return GRAPH * here, GRAPH * there, GRAPH * by_lane(form)

    def scatter(here, there, meanwhile, x_ref, yp_ref, z_ref, y_ref, xp_send, xp_recv, z_send, z_recv):
        copies = []
        for n, o in enumerate(far + [0]):
            p = chip(o)
            block = p * 2 + 1 - my_core
            value = summed(block) + jnp.where(block == me + 1, there, 0.0)
            x_ref[pl.ds(p, 1)] = value.astype(bf16)[None]
            copies.append(
                remote(x_ref.at[p], yp_ref.at[p], xp_send.at[n], xp_recv.at[p], {"col": partner})
            )
        copies += meanwhile()
        for n, o in enumerate(far):
            p = chip(o)
            value = summed(p * 2 + my_core)
            arrived(yp_ref.at[p], xp_recv.at[p])
            z_ref[pl.ds(p, 1)] = (value + yp_ref[p].astype(f32)).astype(bf16)[None]
            copies.append(
                remote(
                    z_ref.at[p],
                    y_ref.at[my_chip],
                    z_send.at[n],
                    z_recv.at[my_chip],
                    {"col": p * 2 + my_core},
                )
            )
        arrived(yp_ref.at[my_chip], xp_recv.at[my_chip])
        return summed(me) + here + yp_ref[my_chip].astype(f32), copies

    def total(own, y_ref, z_recv):
        for o in near:
            p = chip(o)
            arrived(y_ref.at[p], z_recv.at[p])
            own = own + y_ref[p].astype(f32)
        return own

    def share(p_ref, value, send, recv):
        p_ref[pl.ds(me, 1)] = value[None]
        return [
            remote(
                p_ref.at[me],
                p_ref.at[me],
                send.at[o],
                recv.at[me],
                {"col": lax.rem(me + o, cols)},
            )
            for o in sorted(range(1, cols), key=lambda o: -min(o, cols - o))
        ]

    def all_shares(p_ref, recv):
        for o in range(1, cols):
            other = lax.rem(me + o, cols)
            arrived(p_ref.at[other], recv.at[other])
        return jnp.sum(p_ref[...], axis=0)

    finish(r1_ref, g1_recv)
    here, there, near_form = graph(r1_ref)
    halves(r1_ref)

    def meanwhile():
        norm = by_lane(rhs * rhs)
        form = jnp.zeros(rhs.shape, f32)
        for u in range(cols):
            form = form + r1_ref[u].astype(f32) * summed(u)
        form = by_lane(form) + near_form + RIDGE * norm
        return share(p1_ref, pack(norm, form), p1_send, p1_recv)

    own, copies = scatter(
        here, there, meanwhile, x1_ref, yp1_ref, z1_ref, y1_ref, xp1_send, xp1_recv, z1_send, z1_recv
    )
    sent += copies
    norm_row, form_row = unpack(all_shares(p1_ref, p1_recv))
    shift = jnp.where(norm_row > 0.0, form_row / jnp.where(norm_row > 0.0, norm_row, 1.0), 0.0)
    w = total(own, y1_ref, z1_recv) + RIDGE * rhs

    v = w - shift * rhs
    r2_ref[pl.ds(me, 1)] = v.astype(bf16)[None]
    sent += gather(r2_ref, g2_send, g2_recv)
    square = by_lane(w * w)
    for n in range(chips - 1):
        sent.append(pass_on(n, r2_ref, g2_send, g2_recv))
    finish(r2_ref, g2_recv)
    here, there, form = graph(r2_ref)
    form = form + by_lane(first_half(r2_ref)) + RIDGE * by_lane(v * v)
    sent += share(p2_ref, pack(square, form), p2_send, p2_recv)
    second_half()
    own, copies = scatter(
        here, there, list, x2_ref, yp2_ref, z2_ref, y2_ref, xp2_send, xp2_recv, z2_send, z2_recv
    )
    sent += copies
    square_row, bent_row = unpack(all_shares(p2_ref, p2_recv))
    cubic_row = bent_row + 2.0 * shift * square_row - shift * shift * form_row
    line = jnp.where(lane < 64, square_row, cubic_row)
    line = jnp.where(lane == 0, norm_row, jnp.where(lane == 1, form_row, line))
    p3_ref[pl.ds(my_row, 1)] = line[None]
    for o in range(1, rows):
        sent.append(
            remote(
                p3_ref.at[my_row],
                p3_ref.at[my_row],
                p3_send.at[o - 1],
                p3_recv.at[my_row],
                {"row": lax.rem(my_row + o, rows)},
            )
        )
    hv = total(own, y2_ref, z2_recv) + RIDGE * v
    z = hv + shift * w
    for copy in sent:
        copy.wait_send()
    for o in range(1, rows):
        other = lax.rem(my_row + o, rows)
        arrived(p3_ref.at[other], p3_recv.at[other])
    line = jnp.sum(p3_ref[...], axis=0)
    norm0, form1, square1, cubic1 = (
        over_lanes(jnp.where(lane == n, line, 0.0)) for n in (0, 1, 2, 64)
    )
    alpha1 = norm0 / form1
    norm1 = norm0 - 2.0 * alpha1 * form1 + alpha1 * alpha1 * square1
    more = 1.0 + norm1 / norm0
    curve = more * more * form1 - 2.0 * more * alpha1 * square1 + alpha1 * alpha1 * cubic1
    alpha2 = norm1 / curve
    plus, cross = alpha1 + alpha2 * more, alpha1 * alpha2
    out_ref[0] = (plus - 1.0) * rhs - cross * w
    out_ref[1] = cross * z - plus * w


def per_device(rows, cols, *args):
    rhs, items, users, slot_items, counts, words, selfs, nexts = args
    slots = users.shape[2]
    blocks, rank, width = items.shape
    chips = cols // 2
    vmem = pl.BlockSpec(memory_space=pltpu.VMEM)
    hbm = pl.BlockSpec(memory_space=pltpu.HBM)
    dma = pltpu.SemaphoreType.DMA
    half = pltpu.VMEM((chips, rank, width), bf16)
    out = pl.pallas_call(
        functools.partial(kernel, rows, cols),
        out_shape=jax.ShapeDtypeStruct((2, rank, width), f32),
        in_specs=[hbm] * 8,
        out_specs=vmem,
        scratch_shapes=[
            pltpu.VMEM((rank, width), f32),
            pltpu.VMEM((1, slots), i32),
            pltpu.VMEM((1, slots), i32),
            pltpu.VMEM((1, 1), i32),
            pltpu.VMEM((blocks, rank, width), bf16),
            pltpu.VMEM((blocks, width, rank), bf16),
            pltpu.VMEM((slots, width // 8, width), i32),
            pltpu.VMEM((slots, width, width), bf16),
            pltpu.VMEM((slots, width, width), bf16),
            pltpu.VMEM((slots + 1, rank, width), f32),
            pltpu.VMEM((cols + 1, rank, width), bf16),
            pltpu.VMEM((cols + 1, rank, width), bf16),
            *[half] * 8,
            pltpu.VMEM((width, width), i32),
            pltpu.VMEM((width, width), i32),
            pltpu.VMEM((width, width), bf16),
            pltpu.VMEM((width, width), bf16),
            pltpu.VMEM((width, width), bf16),
            pltpu.VMEM((8, 128), i32),
            pltpu.SMEM((8, 128), i32),
            pltpu.VMEM((cols, 1, 128), f32),
            pltpu.VMEM((cols, 1, 128), f32),
            pltpu.VMEM((rows, 1, 128), f32),
            dma((9,)),
            *[dma((cols,))] * 8,
            *[dma((chips,))] * 8,
            dma((rows,)),
            dma((rows,)),
        ],
        compiler_params=pltpu.CompilerParams(collective_id=0, has_side_effects=True),
        name="cg",
    )(*args)
    return out[0:1] + rhs, out[1:2] + rhs


def solution(mesh):
    rows, cols = mesh.shape["row"], mesh.shape["col"]
    user_blocks = P(("row", "col"), None, None)
    return jax.shard_map(
        functools.partial(per_device, rows, cols),
        mesh=mesh,
        in_specs=(
            user_blocks,
            P("col", None, None),
            P("row", "col", None),
            P("row", "col", None),
            P("row", "col"),
            P("row", "col", None, None, None),
            user_blocks,
            user_blocks,
        ),
        out_specs=(user_blocks, user_blocks),
        check_vma=False,
    )
```
